32 devices in a mesh: groups: 2 (over y), seq: 4 (over z), chan: 2 (over x), sub: 2 (over core).
Axes of the slice: x: 2, y: 2, z: 4, core: 2. Of those that a mesh axis runs over, the one named last changes fastest.
Arguments:
- tokens: bfloat16 [16384, 2048], P(('groups', 'seq', 'sub'), 'chan'), parts along dimension 0, may hold values from -6 to 6
- low_angle: float32 [2048], P('chan'), may hold values from 0.1 to 1.47
- high_taps: float32 [2, 2048], P(None, 'chan'), may hold values from -3 to 3
- level_mix: float32 [17, 2048], P(None, 'chan'), may hold values from -1.5 to 1.5
- w_value: bfloat16 [2048, 2048], P(None, 'chan'), may hold values from -0.125 to 0.125
- w_gate: bfloat16 [2048, 2048], P(None, 'chan'), may hold values from -0.125 to 0.125
- out_weight: bfloat16 [2048, 2048], P(None, 'chan'), may hold values from -0.125 to 0.125
Outputs:
- result: bfloat16 [16384, 2048], P(('groups', 'seq', 'sub'), 'chan'), parts along dimension 0
The draws below stay inside these ranges and needn't reach their ends.
There are 2 independent parts, one for each index of `groups`. The reference program is written for one: setup_inputs(seed, part) draws one part's arguments, and reference() takes and returns one part's arrays. A program takes and returns all parts, laid end to end along the dimension named above; an argument that names none is the same for every part. Nothing has to cross between parts.
All inputs are finite; a program needn't handle non-finite values.
Results may differ from the reference program's by a relative error of at most 0.0043.
Values may be sent and summed in bfloat16 or wider, within the bound.
A program may use at most 128 MiB of HBM per device.

```python
import jax
import jax.numpy as jnp
from jax import lax

D = 2048
LEVELS = 15
TOKENS = 8192


def level_of(key, extent, cuts, least, top_value):
    gain = 1.0
    for axis_at, blocks in cuts:
        steps = jax.random.uniform(jax.random.fold_in(jax.random.fold_in(key, 6), axis_at), (blocks,), jnp.float32, least / len(cuts), top_value / len(cuts))
        gain = gain * jnp.repeat(jnp.exp(steps), extent[axis_at] // blocks).reshape((-1,) + (1,) * (len(extent) - 1 - axis_at))
    return gain


def noise(own_key, dims, scale, most, cuts=(), dtype=jnp.bfloat16):
    drawn = scale * jax.random.normal(own_key, dims, jnp.float32)
    if cuts:
        drawn = drawn * level_of(own_key, dims, cuts, -0.22, 0.18)
    return jnp.clip(drawn, -most, most).astype(dtype)


def setup_inputs(seed: int = 0, part: int = 0) -> dict:
    keys = jax.random.split(jax.random.key(seed), 8)
    part_splits = jax.random.split(jax.random.fold_in(keys[7], part), 8)
    return {
        "tokens": noise(part_splits[0], (TOKENS, D), 1.0, 6.0, ((0, 8), (1, 2))),
        "low_angle": jnp.clip(0.1 + 1.37 * jax.random.uniform(keys[1], (D,), jnp.float32) ** level_of(keys[1], (D,), ((0, 2),), -0.2, 0.2), 0.1, 1.47),
        "high_taps": noise(keys[2], (2, D), 0.7, 3.0, ((1, 2),), jnp.float32),
        "level_mix": noise(keys[3], (LEVELS + 2, D), (LEVELS + 2) ** -0.5, 1.5, ((1, 2),), jnp.float32),
        "w_value": noise(keys[4], (D, D), D ** -0.5, 0.125, ((1, 2),)),
        "w_gate": noise(keys[5], (D, D), D ** -0.5, 0.125, ((1, 2),)),
        "out_weight": noise(keys[6], (D, D), D ** -0.5, 0.125, ((1, 2),)),
    }


def filter_block(inputs):
    block, angle, high_pair, mix = inputs
    low0 = jnp.cos(angle)
    low1 = jnp.sin(angle)
    stream = block.astype(jnp.float32)
    length = stream.shape[0]
    mixed = mix[LEVELS + 1] * stream
    for level in range(LEVELS):
        reach = 2 ** level
        if reach < length:
            shifted = jnp.concatenate([jnp.zeros((reach, stream.shape[1]), jnp.float32), stream[:length - reach]], 0)
        else:
            shifted = jnp.zeros_like(stream)
        high = high_pair[0] * stream + high_pair[1] * shifted
        stream = low0 * stream + low1 * shifted
        mixed = mixed + mix[level] * high
    mixed = mixed + mix[LEVELS] * stream
    return jax.nn.gelu(mixed).astype(jnp.bfloat16)


def reference(tokens, low_angle, high_taps, level_mix, w_value, w_gate, out_weight):
    length = tokens.shape[0]
    width = tokens.shape[1]
    blocks = width // 256
    tok_blocks = tokens.reshape(length, blocks, 256).transpose(1, 0, 2)
    angle_blocks = low_angle.reshape(blocks, 256)
    high_blocks = high_taps.reshape(2, blocks, 256).transpose(1, 0, 2)
    mix_blocks = level_mix.reshape(LEVELS + 2, blocks, 256).transpose(1, 0, 2)
    activated = lax.map(filter_block, (tok_blocks, angle_blocks, high_blocks, mix_blocks))
    activated = activated.transpose(1, 0, 2).reshape(length, width)
    value = jnp.dot(activated, w_value, preferred_element_type=jnp.float32)
    gate = jnp.dot(activated, w_gate, preferred_element_type=jnp.float32)
    hidden = (value * jax.nn.sigmoid(gate)).astype(jnp.bfloat16)
    outcome = jnp.dot(hidden, out_weight, preferred_element_type=jnp.float32) + tokens.astype(jnp.float32)
    return outcome.astype(jnp.bfloat16)
```

```python
import functools

import jax
import jax.numpy as jnp
from jax import lax
from jax.experimental import pallas as pl
from jax.experimental.pallas import tpu as pltpu
from jax.sharding import PartitionSpec as P

MESH = pl.DeviceIdType.MESH
F32 = jnp.float32
BF16 = jnp.bfloat16
LANES = 128
STEP = 128
TILE = 512
PIECES = 4
SINGLE = 6
AHEAD = 4
EIGHTHS = (2, 2, 2, 1, 1)


def run_levels(stream, shifter, low0, low1, high0, high1, mix):
    levels = mix.shape[0] - 2
    mixed = mix[levels + 1] * stream
    for level in range(levels):
        shifted = shifter(stream, 2**level)
        high = high0 * stream + high1 * shifted
        stream = low0 * stream + low1 * shifted
        mixed = mixed + mix[level] * high
    return mixed + mix[levels] * stream


def plain(tokens, low_angle, high_taps, level_mix, w_value, w_gate, out_weight):
    rows = tokens.shape[0]
    channels = tokens.shape[1]
    ways = lax.axis_size(("seq", "sub"))
    total = rows * ways
    narrow = channels // ways
    place = lax.axis_index(("seq", "sub")) * narrow
    columns = lax.all_to_all(tokens.T, ("seq", "sub"), split_axis=0, concat_axis=1, tiled=True)
    angle = lax.dynamic_slice_in_dim(low_angle, place, narrow, 0)[:, None]
    high_pair = lax.dynamic_slice_in_dim(high_taps, place, narrow, 1)[:, :, None]
    mix = lax.dynamic_slice_in_dim(level_mix, place, narrow, 1)[:, :, None]

    def shifter(stream, reach):
        if reach >= total:
            return jnp.zeros_like(stream)
        return jnp.concatenate(
            [jnp.zeros((stream.shape[0], reach), F32), stream[:, : total - reach]], 1
        )

    mixed = run_levels(
        columns.astype(F32),
        shifter,
        jnp.cos(angle),
        jnp.sin(angle),
        high_pair[0],
        high_pair[1],
        mix,
    )
    filtered = jax.nn.gelu(mixed).astype(BF16)
    activated = lax.all_to_all(filtered, ("seq", "sub"), split_axis=1, concat_axis=0, tiled=True).T
    piece = lax.all_gather(activated, "chan", axis=1, tiled=True)
    value = jnp.dot(piece, w_value, preferred_element_type=F32)
    gate = jnp.dot(piece, w_gate, preferred_element_type=F32)
    hidden = (value * jax.nn.sigmoid(gate)).astype(BF16)
    projected = jnp.dot(
        lax.all_gather(hidden, "chan", axis=1, tiled=True),
        out_weight,
        preferred_element_type=F32,
    )
    return (projected + tokens.astype(F32)).astype(BF16)


def kernel(
    ways,
    tokens,
    low_angle,
    high_taps,
    level_mix,
    w_value,
    w_gate,
    out_weight,
    out,
    toks,
    cols,
    hist,
    near,
    coef,
    act,
    piece,
    hid,
    wbuf,
    obuf,
    rbuf,
    done,
    local_sem,
    in_send,
    in_recv,
    w_send,
    wx_recv,
    wz_recv,
    wy_recv,
    wc_recv,
    act_send,
    act_recv,
    res_send,
    res_recv,
    out_sem,
):
    rows, half = tokens.shape
    total = rows * ways
    levels = level_mix.shape[0] - 2
    subs = 2
    y = lax.axis_index("groups")
    z = lax.axis_index("seq")
    x = lax.axis_index("chan")
    u = lax.axis_index("sub")
    me = z * subs + u
    nx, ny, nu = 1 - x, 1 - y, 1 - u
    low = lax.rem(z, 2)
    nz = z + 1 - 2 * low
    part = rows // 2
    sizes = [part // 8 * e for e in EIGHTHS]
    starts = [sum(sizes[:q]) for q in range(len(sizes))]
    chunks = len(sizes)
    depth = wbuf.shape[2]
    ws = (w_value, w_gate, out_weight)

    barrier = pltpu.get_barrier_semaphore()
    for other in range(1, 2 * ways):
        them = lax.rem(me * 2 + x + other, 2 * ways)
        pl.semaphore_signal(
            barrier,
            inc=1,
            device_id={"seq": them // 4, "sub": lax.rem(them // 2, 2), "chan": lax.rem(them, 2)},
            device_id_type=MESH,
        )
    pl.semaphore_signal(barrier, inc=1, device_id={"groups": ny}, device_id_type=MESH)

    own_in = pltpu.make_async_copy(
        tokens.at[:, pl.ds(pl.multiple_of(me * LANES, LANES), LANES)],
        cols.at[pl.ds(pl.multiple_of(me * rows, rows), rows)],
        in_recv.at[me],
    )
    own_in.start()
    load = pltpu.make_async_copy(tokens, toks, local_sem.at[3])
    load.start()
    own_w = [pltpu.make_async_copy(ws[i], wbuf.at[i, x], local_sem.at[i]) for i in range(3)]
    for copy in own_w:
        copy.start()

    @pl.loop(0, total // STEP)
    def _(i):
        hist[pl.ds(pl.multiple_of(i * STEP, STEP), STEP)] = jnp.zeros((STEP, LANES), F32)

    near[...] = jnp.zeros_like(near)

    lanes = pl.ds(pl.multiple_of(me * LANES, LANES), LANES)
    angle = low_angle[0:1, lanes]
    low0, low1 = jnp.cos(angle), jnp.sin(angle)
    high0, high1 = high_taps[0:1, lanes], high_taps[1:2, lanes]
    mix = [level_mix[k : k + 1, lanes] for k in range(levels + 2)]
    slope = low0 / low1
    stay, step_up = high0 - high1 * slope, high1 / low1
    live = sum(2**k < total for k in range(levels))
    weights = [mix[levels + 1] + mix[0] * stay]
    scale = low0
    for k in range(1, levels + 1):
        weight = mix[k - 1] * step_up + (mix[k] * stay if k < levels else mix[k])
        weights.append(weight * scale)
        scale = scale * low0
    last = weights[live]
    for k in range(live + 1, levels + 1):
        last = last + weights[k]
    for k in range(live):
        coef[k : k + 1] = weights[k]
    coef[live : live + 1] = last
    coef[live + 1 : live + 2] = low1 / low0

    pl.semaphore_wait(barrier, 2 * ways)

    def in_copy(peer, source):
        columns = pl.ds(pl.multiple_of(peer * LANES, LANES), LANES)
        return pltpu.make_async_remote_copy(
            src_ref=tokens.at[:, columns],
            dst_ref=cols.at[pl.ds(pl.multiple_of(source * rows, rows), rows)],
            send_sem=in_send,
            recv_sem=in_recv.at[source],
            device_id={"seq": peer // subs, "sub": lax.rem(peer, subs)},
            device_id_type=MESH,
        )

    for other in range(1, ways):
        in_copy(lax.rem(me + other, ways), me).start()

    count = 3 * PIECES
    first_single = count - SINGLE
    band = depth // PIECES
    quarter = band // 4

    def region(p, group, narrow=None):
        i, k = divmod(p, PIECES)
        base = k * band + (group * 2 + u) * quarter
        if narrow is None:
            return i, pl.ds(pl.multiple_of(base, quarter), quarter)
        fine = quarter // 2
        return i, pl.ds(pl.multiple_of(base + narrow * fine, fine), fine)

    def single(p):
        return p >= first_single

    def x_copy(p):
        i, at = region(p, y, low if single(p) else None)
        return pltpu.make_async_remote_copy(
            src_ref=ws[i].at[at],
            dst_ref=wbuf.at[i, x, at],
            send_sem=w_send.at[0],
            recv_sem=wx_recv.at[p],
            device_id={"chan": nx},
            device_id_type=MESH,
        )

    def w_copy(i, at, sem, target):
        slot = wbuf.at[i, nx, at]
        return pltpu.make_async_remote_copy(
            src_ref=slot,
            dst_ref=slot,
            send_sem=w_send.at[1],
            recv_sem=sem,
            device_id=target,
            device_id_type=MESH,
        )

    def z_copy(p):
        return w_copy(*region(p, y, low), wz_recv.at[p - first_single], {"seq": nz})

    def y_copy(p):
        return w_copy(*region(p, y), wy_recv.at[p], {"groups": ny})

    def c_copy(p, group):
        return w_copy(*region(p, group), wc_recv.at[p], {"sub": nu})

    def whole(p):
        y_copy(p).start()
        c_copy(p, y).start()

    def arrive(p):
        x_copy(p).wait_recv()
        if single(p):
            z_copy(p).start()
        else:
            whole(p)
        if p + AHEAD < count:
            x_copy(p + AHEAD).start()

    def across(p):
        y_copy(p).wait_recv()
        c_copy(p, ny).start()

    def relay(n):
        if n < count:
            arrive(n)
        if single(n - 1) and n - 1 < count:
            z_copy(n - 1).wait_recv()
            whole(n - 1)
        for p in (n - 1, n - 2):
            if 0 <= p < count and single(p) == (p == n - 2):
                across(p)

    for p in range(AHEAD):
        x_copy(p).start()

    def act_copy(owner, h, q, source, source_x):
        start = pl.multiple_of(owner * rows + h * part + starts[q], 16)
        to = pl.ds(pl.multiple_of(source_x * half + source * LANES, LANES), LANES)
        return pltpu.make_async_remote_copy(
            src_ref=act.at[pl.ds(start, sizes[q])],
            dst_ref=piece.at[pl.ds(starts[q], sizes[q]), to],
            send_sem=act_send.at[q],
            recv_sem=act_recv.at[q],
            device_id={"seq": owner // subs, "sub": lax.rem(owner, subs), "chan": h},
            device_id_type=MESH,
        )

    def own_act(q):
        start = pl.multiple_of(me * rows + x * part + starts[q], 16)
        to = pl.ds(pl.multiple_of(x * half + me * LANES, LANES), LANES)
        return pltpu.make_async_copy(
            act.at[pl.ds(start, sizes[q])], piece.at[pl.ds(starts[q], sizes[q]), to], act_recv.at[q]
        )

    def send_act(owner, q):
        for h in range(2):
            mine_too = jnp.logical_and(owner == me, x == h)

            @pl.when(mine_too)
            def _():
                own_act(q).start()

            @pl.when(jnp.logical_not(mine_too))
            def _():
                act_copy(owner, h, q, me, x).start()

    def send_all(q):
        @pl.loop(0, ways)
        def _(other):
            send_act(lax.rem(me + other + ways // 2, ways), q)

    def advance(at):
        s = cols[pl.ds(at, STEP)].astype(F32)
        tan = coef[live + 1 : live + 2]
        m = coef[0:1] * s
        for k in range(live):
            reach = 2**k
            if reach < 8:
                near[k, 8 : 8 + STEP] = s
                d = near[k, 8 - reach : 8 - reach + STEP]
                near[k, 0:8] = s[STEP - 8 :]
            elif reach < STEP:
                d = jnp.concatenate([hist[reach : 2 * reach], s[: STEP - reach]], 0)
                hist[reach : 2 * reach] = s[STEP - reach :]
            else:
                slot = pl.ds(pl.multiple_of(reach + lax.rem(at, reach), STEP), STEP)
                d = hist[slot]
                hist[slot] = s
            s = s + tan * d
            m = m + coef[k + 1 : k + 2] * s
        act[pl.ds(at, STEP)] = jax.nn.gelu(m).astype(BF16)

    left = z < 2
    posts = [(0, 0)] * 5 + [(1, 0), (2, 0), (3, 0), (4, 0), (5, 2), (6, 4), (7, 6)]

    @pl.loop(0, ways)
    def _(block):
        for n, (a, b) in enumerate(posts):
            when = a if a == b else jnp.where(left, a, b)

            @pl.when(block == when)
            def _():
                relay(n)

        @pl.when(block != me)
        def _():
            in_copy(block, block).wait_recv()

        @pl.when(block == me)
        def _():
            own_in.wait()

        @pl.loop(0, rows // STEP)
        def _(i):
            advance(pl.multiple_of(block * rows + i * STEP, STEP))

        send_act(block, 0)

    send_all(1)
    for n in range(len(posts), len(posts) + 2):
        relay(n)

    def wait_bytes(ref, sem):
        pltpu.make_async_copy(ref, ref, sem).wait()

    def weights_here(i):
        own_w[i].wait()
        for p in range(i * PIECES, (i + 1) * PIECES):
            wait_bytes(wbuf.at[i, nx, pl.ds(0, 2 * quarter)], wc_recv.at[p])

    tiles = half // TILE

    def result_copy(q):
        at = pl.ds(starts[q], sizes[q])
        return pltpu.make_async_remote_copy(
            src_ref=obuf.at[at],
            dst_ref=rbuf.at[at],
            send_sem=res_send,
            recv_sem=res_recv.at[q],
            device_id={"chan": nx},
            device_id_type=MESH,
        )

    def out_copy(q, owner):
        at = pl.ds(pl.multiple_of(owner * part + starts[q], 16), sizes[q])
        return pltpu.make_async_copy(done.at[at], out.at[at], out_sem)

    def widen(q):
        at = pl.ds(starts[q], sizes[q])
        wait_bytes(piece.at[at], act_recv.at[q])
        if q + 2 < chunks:
            send_all(q + 2)
        if q == 0:
            weights_here(0)
            weights_here(1)

        for h in range(2):

            @pl.loop(0, tiles)
            def _(tile):
                lanes = pl.ds(pl.multiple_of(tile * TILE, TILE), TILE)
                value = jnp.dot(piece[at], wbuf[0, h, :, lanes], preferred_element_type=F32)
                gate = jnp.dot(piece[at], wbuf[1, h, :, lanes], preferred_element_type=F32)
                to = pl.ds(pl.multiple_of(h * half + tile * TILE, TILE), TILE)
                hid[0 : sizes[q], to] = (value * jax.nn.sigmoid(gate)).astype(BF16)

    def project(q):
        @pl.loop(0, tiles)
        def _(tile):
            lanes = pl.ds(pl.multiple_of(tile * TILE, TILE), TILE)
            obuf[starts[q] : starts[q] + sizes[q], lanes] = jnp.dot(
                hid[0 : sizes[q]], wbuf[2, nx, :, lanes], preferred_element_type=F32
            ).astype(BF16)

        result_copy(q).start()
        at = pl.ds(pl.multiple_of(x * part + starts[q], 16), sizes[q])

        @pl.loop(0, tiles)
        def _(tile):
            lanes = pl.ds(pl.multiple_of(tile * TILE, TILE), TILE)
            projected = jnp.dot(hid[0 : sizes[q]], wbuf[2, x, :, lanes], preferred_element_type=F32)
            done[at, lanes] = (projected + toks[at, lanes].astype(F32)).astype(BF16)

        out_copy(q, x).start()

    def finish(q):
        result_copy(q).wait_recv()
        base = nx * part + starts[q]

        @pl.loop(0, sizes[q] // 16)
        def _(i):
            at = pl.ds(pl.multiple_of(base + i * 16, 16), 16)
            got = rbuf[pl.ds(pl.multiple_of(starts[q] + i * 16, 16), 16)].astype(F32)
            done[at] = (got + toks[at].astype(F32)).astype(BF16)

        out_copy(q, nx).start()

    for q in range(chunks):
        widen(q)
        if q == 0:
            load.wait()
            weights_here(2)
        project(q)
        if q > 0:
            finish(q - 1)
    finish(chunks - 1)

    wait_bytes(cols.at[pl.ds(0, (ways - 1) * rows)], in_send)
    for p in range(count):
        x_copy(p).wait_send()
        if single(p):
            z_copy(p).wait_send()
        y_copy(p).wait_send()
        c_copy(p, y).wait_send()
        c_copy(p, ny).wait_send()
    for q in range(chunks):
        wait_bytes(act.at[pl.ds(0, (2 * ways - 1) * sizes[q])], act_send.at[q])
    wait_bytes(obuf, res_send)
    wait_bytes(done, out_sem)


def fused(tokens, low_angle, high_taps, level_mix, w_value, w_gate, out_weight):
    rows, half = tokens.shape
    depth = w_value.shape[0]
    ways = lax.axis_size(("seq", "sub"))
    total = rows * ways
    part = rows // 2
    chunk = part // 8 * max(EIGHTHS)
    chunks = len(EIGHTHS)
    vmem = pl.BlockSpec(memory_space=pltpu.VMEM)
    hbm = pl.BlockSpec(memory_space=pl.ANY)
    dma = pltpu.SemaphoreType.DMA
    return pl.pallas_call(
        functools.partial(kernel, ways),
        out_shape=jax.ShapeDtypeStruct((rows, half), BF16),
        in_specs=[hbm, vmem, vmem, vmem, hbm, hbm, hbm],
        out_specs=hbm,
        scratch_shapes=[
            pltpu.VMEM((rows, half), BF16),
            pltpu.VMEM((total, LANES), BF16),
            pltpu.VMEM((total, LANES), F32),
            pltpu.VMEM((3, STEP + 8, LANES), F32),
            pltpu.VMEM((level_mix.shape[0] + 7, LANES), F32),
            pltpu.VMEM((total, LANES), BF16),
            pltpu.VMEM((part, depth), BF16),
            pltpu.VMEM((chunk, depth), BF16),
            pltpu.VMEM((3, 2, depth, half), BF16),
            pltpu.VMEM((part, half), BF16),
            pltpu.VMEM((part, half), BF16),
            pltpu.VMEM((rows, half), BF16),
            dma((4,)),
            dma(()),
            dma((ways,)),
            dma((2,)),
            dma((3 * PIECES,)),
            dma((SINGLE,)),
            dma((3 * PIECES,)),
            dma((3 * PIECES,)),
            dma((chunks,)),
            dma((chunks,)),
            dma(()),
            dma((chunks,)),
            dma(()),
        ],
        compiler_params=pltpu.CompilerParams(
            collective_id=0, has_side_effects=True, vmem_limit_bytes=60 * 1024 * 1024
        ),
        name="layer",
    )(tokens, low_angle[None], high_taps, level_mix, w_value, w_gate, out_weight)


def solution(mesh):
    shape = mesh.shape
    pair = shape["groups"] == 2 and shape["chan"] == 2 and shape["sub"] == 2 and shape["seq"] == 4
    ways = shape["seq"] * shape["sub"]

    def shards(tokens, *rest):
        rows, half = tokens.shape
        fits = half == ways * LANES and rows % STEP == 0 and rows % 256 == 0 and half % TILE == 0
        whole = rest[3].shape[0] == 2 * half and rows * ways * LANES <= 1 << 20
        body = fused if pair and fits and whole else plain
        return body(tokens, *rest)

    return jax.shard_map(
        shards,
        mesh=mesh,
        in_specs=(
            P(("groups", "seq", "sub"), "chan"),
            P("chan"),
            P(None, "chan"),
            P(None, "chan"),
            P(None, "chan"),
            P(None, "chan"),
            P(None, "chan"),
        ),
        out_specs=P(("groups", "seq", "sub"), "chan"),
        check_vma=False,
    )
```

```python
import functools

import jax
import jax.numpy as jnp
from jax import lax
from jax.experimental import pallas as pl
from jax.experimental.pallas import tpu as pltpu
from jax.sharding import PartitionSpec as P

MESH = pl.DeviceIdType.MESH
F32 = jnp.float32
BF16 = jnp.bfloat16
LANES = 128
STEP = 128
TILE = 512
PIECES = 4
OVER_Y = (None, "groups")
OVER_Z = (None, "seq")
ZY = ("seq", "groups")
YZ = ("groups", "seq")
HOPS = (YZ,) * 4 + (OVER_Y,) * 8
N = None
BEFORE = ((0, N, N), (1, 0, N), (2, 1, N), (3, 2, N), (4, 3, N), (5, N, 4), (6, N, 5))
DURING = ((1, 0, ((7, N, 6),)), (3, 0, ((8, N, 7),)), (6, 4, ((9, N, 8),)))
AFTER = ((10, N, 9), (N, N, 0), (N, N, 1), (N, N, 2), (N, N, 3), (11, N, 10), (N, N, 11))
EARLY = 1
DEEP = 3
AHEAD = 4
EIGHTHS = (2, 2, 2, 1, 1)


def run_levels(stream, shifter, low0, low1, high0, high1, mix):
    levels = mix.shape[0] - 2
    mixed = mix[levels + 1] * stream
    for level in range(levels):
        shifted = shifter(stream, 2**level)
        high = high0 * stream + high1 * shifted
        stream = low0 * stream + low1 * shifted
        mixed = mixed + mix[level] * high
    return mixed + mix[levels] * stream


def plain(tokens, low_angle, high_taps, level_mix, w_value, w_gate, out_weight):
    rows = tokens.shape[0]
    channels = tokens.shape[1]
    ways = lax.axis_size(("seq", "sub"))
    total = rows * ways
    narrow = channels // ways
    place = lax.axis_index(("seq", "sub")) * narrow
    columns = lax.all_to_all(tokens.T, ("seq", "sub"), split_axis=0, concat_axis=1, tiled=True)
    angle = lax.dynamic_slice_in_dim(low_angle, place, narrow, 0)[:, None]
    high_pair = lax.dynamic_slice_in_dim(high_taps, place, narrow, 1)[:, :, None]
    mix = lax.dynamic_slice_in_dim(level_mix, place, narrow, 1)[:, :, None]

    def shifter(stream, reach):
        if reach >= total:
            return jnp.zeros_like(stream)
        return jnp.concatenate(
            [jnp.zeros((stream.shape[0], reach), F32), stream[:, : total - reach]], 1
        )

    mixed = run_levels(
        columns.astype(F32),
        shifter,
        jnp.cos(angle),
        jnp.sin(angle),
        high_pair[0],
        high_pair[1],
        mix,
    )
    filtered = jax.nn.gelu(mixed).astype(BF16)
    activated = lax.all_to_all(filtered, ("seq", "sub"), split_axis=1, concat_axis=0, tiled=True).T
    piece = lax.all_gather(activated, "chan", axis=1, tiled=True)
    value = jnp.dot(piece, w_value, preferred_element_type=F32)
    gate = jnp.dot(piece, w_gate, preferred_element_type=F32)
    hidden = (value * jax.nn.sigmoid(gate)).astype(BF16)
    projected = jnp.dot(
        lax.all_gather(hidden, "chan", axis=1, tiled=True),
        out_weight,
        preferred_element_type=F32,
    )
    return (projected + tokens.astype(F32)).astype(BF16)


def kernel(
    ways,
    tokens,
    low_angle,
    high_taps,
    level_mix,
    w_value,
    w_gate,
    out_weight,
    out,
    toks,
    cols,
    hist,
    near,
    coef,
    act,
    piece,
    hid,
    wbuf,
    obuf,
    rbuf,
    done,
    local_sem,
    in_send,
    in_recv,
    w_send,
    wx_recv,
    wa_recv,
    wb_recv,
    wc_recv,
    act_send,
    act_recv,
    res_send,
    res_recv,
    out_sem,
):
    rows, half = tokens.shape
    total = rows * ways
    levels = level_mix.shape[0] - 2
    subs = 2
    y = lax.axis_index("groups")
    z = lax.axis_index("seq")
    x = lax.axis_index("chan")
    u = lax.axis_index("sub")
    me = z * subs + u
    nx, ny, nu = 1 - x, 1 - y, 1 - u
    low = lax.rem(z, 2)
    nz = z + 1 - 2 * low
    part = rows // 2
    sizes = [part // 8 * e for e in EIGHTHS]
    starts = [sum(sizes[:q]) for q in range(len(sizes))]
    chunks = len(sizes)
    depth = wbuf.shape[2]
    ws = (w_value, w_gate, out_weight)

    barrier = pltpu.get_barrier_semaphore()
    for other in range(1, 2 * ways):
        them = lax.rem(me * 2 + x + other, 2 * ways)
        pl.semaphore_signal(
            barrier,
            inc=1,
            device_id={"seq": them // 4, "sub": lax.rem(them // 2, 2), "chan": lax.rem(them, 2)},
            device_id_type=MESH,
        )
    pl.semaphore_signal(barrier, inc=1, device_id={"groups": ny}, device_id_type=MESH)

    own_in = pltpu.make_async_copy(
        tokens.at[:, pl.ds(pl.multiple_of(me * LANES, LANES), LANES)],
        cols.at[pl.ds(pl.multiple_of(me * rows, rows), rows)],
        in_recv.at[me],
    )
    own_in.start()
    load = pltpu.make_async_copy(tokens, toks, local_sem.at[3])
    load.start()
    own_w = [pltpu.make_async_copy(ws[i], wbuf.at[i, x], local_sem.at[i]) for i in range(3)]
    for copy in own_w:
        copy.start()

    @pl.loop(0, total // STEP)
    def _(i):
        hist[pl.ds(pl.multiple_of(i * STEP, STEP), STEP)] = jnp.zeros((STEP, LANES), F32)

    near[...] = jnp.zeros_like(near)

    lanes = pl.ds(pl.multiple_of(me * LANES, LANES), LANES)
    angle = low_angle[0:1, lanes]
    low0, low1 = jnp.cos(angle), jnp.sin(angle)
    high0, high1 = high_taps[0:1, lanes], high_taps[1:2, lanes]
    mix = [level_mix[k : k + 1, lanes] for k in range(levels + 2)]
    slope = low0 / low1
    stay, step_up = high0 - high1 * slope, high1 / low1
    live = sum(2**k < total for k in range(levels))
    weights = [mix[levels + 1] + mix[0] * stay]
    scale = low0
    for k in range(1, levels + 1):
        weight = mix[k - 1] * step_up + (mix[k] * stay if k < levels else mix[k])
        weights.append(weight * scale)
        scale = scale * low0
    last = weights[live]
    for k in range(live + 1, levels + 1):
        last = last + weights[k]
    for k in range(live):
        coef[k : k + 1] = weights[k]
    coef[live : live + 1] = last
    coef[live + 1 : live + 2] = low1 / low0

    pl.semaphore_wait(barrier, 2 * ways)

    def in_copy(peer, source):
        columns = pl.ds(pl.multiple_of(peer * LANES, LANES), LANES)
        return pltpu.make_async_remote_copy(
            src_ref=tokens.at[:, columns],
            dst_ref=cols.at[pl.ds(pl.multiple_of(source * rows, rows), rows)],
            send_sem=in_send,
            recv_sem=in_recv.at[source],
            device_id={"seq": peer // subs, "sub": lax.rem(peer, subs)},
            device_id_type=MESH,
        )

    for other in range(1, ways):
        in_copy(lax.rem(me + other, ways), me).start()

    count = 3 * PIECES
    band = depth // PIECES
    quarter = band // 4
    spot = {"groups": y, "seq": low}
    beside = {"groups": {"groups": ny}, "seq": {"seq": nz}}

    def region(p, side, narrow=None):
        i, k = divmod(p, PIECES)
        base = k * band + (side * 2 + u) * quarter
        if narrow is None:
            return i, pl.ds(pl.multiple_of(base, quarter), quarter)
        fine = quarter // 2
        return i, pl.ds(pl.multiple_of(base + narrow * fine, fine), fine)

    def first_region(p):
        first, second = HOPS[p]
        return region(p, spot[second], spot[first] if first else None)

    def x_copy(p):
        i, at = first_region(p)
        return pltpu.make_async_remote_copy(
            src_ref=ws[i].at[at],
            dst_ref=wbuf.at[i, x, at],
            send_sem=w_send.at[0],
            recv_sem=wx_recv.at[p],
            device_id={"chan": nx},
            device_id_type=MESH,
        )

    def w_copy(i, at, sem, target):
        slot = wbuf.at[i, nx, at]
        return pltpu.make_async_remote_copy(
            src_ref=slot,
            dst_ref=slot,
            send_sem=w_send.at[1],
            recv_sem=sem,
            device_id=target,
            device_id_type=MESH,
        )

    def a_copy(p):
        return w_copy(*first_region(p), wa_recv.at[p], beside[HOPS[p][0]])

    def b_copy(p):
        second = HOPS[p][1]
        return w_copy(*region(p, spot[second]), wb_recv.at[p], beside[second])

    def c_copy(p, other):
        side = spot[HOPS[p][1]]
        return w_copy(*region(p, 1 - side if other else side), wc_recv.at[p], {"sub": nu})

    def forward(p):
        b_copy(p).start()
        c_copy(p, False).start()

    def arrive(p):
        x_copy(p).wait_recv()
        if HOPS[p][0]:
            a_copy(p).start()
        else:
            forward(p)
        if p + AHEAD < count:
            x_copy(p + AHEAD).start()

    def turn(p):
        a_copy(p).wait_recv()
        forward(p)

    def across(p):
        b_copy(p).wait_recv()
        c_copy(p, True).start()

    def relay(steps):
        for step in steps:
            for act_on, p in zip((arrive, turn, across), step):
                if p is not None:
                    act_on(p)

    for p in range(AHEAD):
        x_copy(p).start()

    relay(BEFORE)

    def act_copy(owner, h, q, source, source_x):
        start = pl.multiple_of(owner * rows + h * part + starts[q], 16)
        to = pl.ds(pl.multiple_of(source_x * half + source * LANES, LANES), LANES)
        return pltpu.make_async_remote_copy(
            src_ref=act.at[pl.ds(start, sizes[q])],
            dst_ref=piece.at[pl.ds(starts[q], sizes[q]), to],
            send_sem=act_send.at[q],
            recv_sem=act_recv.at[q],
            device_id={"seq": owner // subs, "sub": lax.rem(owner, subs), "chan": h},
            device_id_type=MESH,
        )

    def own_act(q):
        start = pl.multiple_of(me * rows + x * part + starts[q], 16)
        to = pl.ds(pl.multiple_of(x * half + me * LANES, LANES), LANES)
        return pltpu.make_async_copy(
            act.at[pl.ds(start, sizes[q])], piece.at[pl.ds(starts[q], sizes[q]), to], act_recv.at[q]
        )

    def send_act(owner, q):
        for h in range(2):
            mine_too = jnp.logical_and(owner == me, x == h)

            @pl.when(mine_too)
            def _():
                own_act(q).start()

            @pl.when(jnp.logical_not(mine_too))
            def _():
                act_copy(owner, h, q, me, x).start()

    side = me // (ways // 2)

    def send_far(q):
        @pl.loop(0, ways // 2)
        def _(other):
            spread = lax.rem(me + other, ways // 2)
            send_act((1 - side) * (ways // 2) + spread, q)

    def advance(at):
        s = cols[pl.ds(at, STEP)].astype(F32)
        tan = coef[live + 1 : live + 2]
        m = coef[0:1] * s
        for k in range(live):
            reach = 2**k
            if reach < 8:
                near[k, 8 : 8 + STEP] = s
                d = near[k, 8 - reach : 8 - reach + STEP]
                near[k, 0:8] = s[STEP - 8 :]
            elif reach < STEP:
                d = jnp.concatenate([hist[reach : 2 * reach], s[: STEP - reach]], 0)
                hist[reach : 2 * reach] = s[STEP - reach :]
            else:
                slot = pl.ds(pl.multiple_of(reach + lax.rem(at, reach), STEP), STEP)
                d = hist[slot]
                hist[slot] = s
            s = s + tan * d
            m = m + coef[k + 1 : k + 2] * s
        act[pl.ds(at, STEP)] = jax.nn.gelu(m).astype(BF16)

    left = z < 2

    @pl.loop(0, ways)
    def _(block):
        for a, b, steps in DURING:
            when = a if a == b else jnp.where(left, a, b)

            @pl.when(block == when)
            def _():
                relay(steps)

        @pl.when(block != me)
        def _():
            in_copy(block, block).wait_recv()

        @pl.when(block == me)
        def _():
            own_in.wait()

        @pl.loop(0, rows // STEP)
        def _(i):
            advance(pl.multiple_of(block * rows + i * STEP, STEP))

        for q in range(EARLY):
            send_act(block, q)

        @pl.when(block // (ways // 2) == side)
        def _():
            for q in range(EARLY, chunks):
                send_act(block, q)

    for q in range(EARLY, DEEP):
        send_far(q)
    relay(AFTER)

    def wait_bytes(ref, sem):
        pltpu.make_async_copy(ref, ref, sem).wait()

    def weights_here(i):
        own_w[i].wait()
        for p in range(i * PIECES, (i + 1) * PIECES):
            wait_bytes(wbuf.at[i, nx, pl.ds(0, 2 * quarter)], wc_recv.at[p])

    tiles = half // TILE

    def result_copy(q):
        at = pl.ds(starts[q], sizes[q])
        return pltpu.make_async_remote_copy(
            src_ref=obuf.at[at],
            dst_ref=rbuf.at[at],
            send_sem=res_send,
            recv_sem=res_recv.at[q],
            device_id={"chan": nx},
            device_id_type=MESH,
        )

    def out_copy(q, owner):
        at = pl.ds(pl.multiple_of(owner * part + starts[q], 16), sizes[q])
        return pltpu.make_async_copy(done.at[at], out.at[at], out_sem)

    def widen(q):
        at = pl.ds(starts[q], sizes[q])
        wait_bytes(piece.at[at], act_recv.at[q])
        if q + DEEP < chunks:
            send_far(q + DEEP)
        if q == 0:
            weights_here(0)
            weights_here(1)

        for h in range(2):

            @pl.loop(0, tiles)
            def _(tile):
                lanes = pl.ds(pl.multiple_of(tile * TILE, TILE), TILE)
                value = jnp.dot(piece[at], wbuf[0, h, :, lanes], preferred_element_type=F32)
                gate = jnp.dot(piece[at], wbuf[1, h, :, lanes], preferred_element_type=F32)
                to = pl.ds(pl.multiple_of(h * half + tile * TILE, TILE), TILE)
                hid[0 : sizes[q], to] = (value * jax.nn.sigmoid(gate)).astype(BF16)

    def project(q):
        @pl.loop(0, tiles)
        def _(tile):
            lanes = pl.ds(pl.multiple_of(tile * TILE, TILE), TILE)
            obuf[starts[q] : starts[q] + sizes[q], lanes] = jnp.dot(
                hid[0 : sizes[q]], wbuf[2, nx, :, lanes], preferred_element_type=F32
            ).astype(BF16)

        result_copy(q).start()
        at = pl.ds(pl.multiple_of(x * part + starts[q], 16), sizes[q])

        @pl.loop(0, tiles)
        def _(tile):
            lanes = pl.ds(pl.multiple_of(tile * TILE, TILE), TILE)
            projected = jnp.dot(hid[0 : sizes[q]], wbuf[2, x, :, lanes], preferred_element_type=F32)
            done[at, lanes] = (projected + toks[at, lanes].astype(F32)).astype(BF16)

        out_copy(q, x).start()

    def finish(q):
        result_copy(q).wait_recv()
        base = nx * part + starts[q]

        @pl.loop(0, sizes[q] // 16)
        def _(i):
            at = pl.ds(pl.multiple_of(base + i * 16, 16), 16)
            got = rbuf[pl.ds(pl.multiple_of(starts[q] + i * 16, 16), 16)].astype(F32)
            done[at] = (got + toks[at].astype(F32)).astype(BF16)

        out_copy(q, nx).start()

    for q in range(chunks):
        widen(q)
        if q == 0:
            load.wait()
            weights_here(2)
        project(q)
        if q > 0:
            finish(q - 1)
    finish(chunks - 1)

    wait_bytes(cols.at[pl.ds(0, (ways - 1) * rows)], in_send)
    for p in range(count):
        x_copy(p).wait_send()
        if HOPS[p][0]:
            a_copy(p).wait_send()
        b_copy(p).wait_send()
        c_copy(p, False).wait_send()
        c_copy(p, True).wait_send()
    for q in range(chunks):
        wait_bytes(act.at[pl.ds(0, (2 * ways - 1) * sizes[q])], act_send.at[q])
    wait_bytes(obuf, res_send)
    wait_bytes(done, out_sem)


def fused(tokens, low_angle, high_taps, level_mix, w_value, w_gate, out_weight):
    rows, half = tokens.shape
    depth = w_value.shape[0]
    ways = lax.axis_size(("seq", "sub"))
    total = rows * ways
    part = rows // 2
    chunk = part // 8 * max(EIGHTHS)
    chunks = len(EIGHTHS)
    vmem = pl.BlockSpec(memory_space=pltpu.VMEM)
    hbm = pl.BlockSpec(memory_space=pl.ANY)
    dma = pltpu.SemaphoreType.DMA
    return pl.pallas_call(
        functools.partial(kernel, ways),
        out_shape=jax.ShapeDtypeStruct((rows, half), BF16),
        in_specs=[hbm, vmem, vmem, vmem, hbm, hbm, hbm],
        out_specs=hbm,
        scratch_shapes=[
            pltpu.VMEM((rows, half), BF16),
            pltpu.VMEM((total, LANES), BF16),
            pltpu.VMEM((total, LANES), F32),
            pltpu.VMEM((3, STEP + 8, LANES), F32),
            pltpu.VMEM((level_mix.shape[0] + 7, LANES), F32),
            pltpu.VMEM((total, LANES), BF16),
            pltpu.VMEM((part, depth), BF16),
            pltpu.VMEM((chunk, depth), BF16),
            pltpu.VMEM((3, 2, depth, half), BF16),
            pltpu.VMEM((part, half), BF16),
            pltpu.VMEM((part, half), BF16),
            pltpu.VMEM((rows, half), BF16),
            dma((4,)),
            dma(()),
            dma((ways,)),
            dma((2,)),
            dma((3 * PIECES,)),
            dma((3 * PIECES,)),
            dma((3 * PIECES,)),
            dma((3 * PIECES,)),
            dma((chunks,)),
            dma((chunks,)),
            dma(()),
            dma((chunks,)),
            dma(()),
        ],
        compiler_params=pltpu.CompilerParams(
            collective_id=0, has_side_effects=True, vmem_limit_bytes=60 * 1024 * 1024
        ),
        name="layer",
    )(tokens, low_angle[None], high_taps, level_mix, w_value, w_gate, out_weight)


def solution(mesh):
    shape = mesh.shape
    pair = shape["groups"] == 2 and shape["chan"] == 2 and shape["sub"] == 2 and shape["seq"] == 4
    ways = shape["seq"] * shape["sub"]

    def shards(tokens, *rest):
        rows, half = tokens.shape
        fits = half == ways * LANES and rows % STEP == 0 and rows % 256 == 0 and half % TILE == 0
        whole = rest[3].shape[0] == 2 * half and rows * ways * LANES <= 1 << 20
        body = fused if pair and fits and whole else plain
        return body(tokens, *rest)

    return jax.shard_map(
        shards,
        mesh=mesh,
        in_specs=(
            P(("groups", "seq", "sub"), "chan"),
            P("chan"),
            P(None, "chan"),
            P(None, "chan"),
            P(None, "chan"),
            P(None, "chan"),
            P(None, "chan"),
        ),
        out_specs=P(("groups", "seq", "sub"), "chan"),
        check_vma=False,
    )
```

```python
import functools

import jax
import jax.numpy as jnp
from jax import lax
from jax.experimental import pallas as pl
from jax.experimental.pallas import tpu as pltpu
from jax.sharding import PartitionSpec as P

MESH = pl.DeviceIdType.MESH
F32 = jnp.float32
BF16 = jnp.bfloat16
LANES = 128
STEP = 128
TILE = 512
PIECES = 4
OVER_Y = (None, "groups")
OVER_Z = (None, "seq")
ZY = ("seq", "groups")
YZ = ("groups", "seq")
HOPS = (YZ,) * 4 + (OVER_Y,) * 8
N = None
BEFORE = ((0, N, N), (1, 0, N), (2, 1, N), (3, 2, N), (4, 3, N), (5, N, 4), (6, N, 5))
DURING = ((1, 0, ((7, N, 6),)), (3, 0, ((8, N, 7),)), (6, 4, ((9, N, 8),)))
AFTER = ((10, N, 9), (N, N, 0), (N, N, 1), (N, N, 2), (N, N, 3), (11, N, 10), (N, N, 11))
EARLY = 1
DEEP = 3
WHOLE = 2
AHEAD = 4
EIGHTHS = (2, 2, 2, 2)


def run_levels(stream, shifter, low0, low1, high0, high1, mix):
    levels = mix.shape[0] - 2
    mixed = mix[levels + 1] * stream
    for level in range(levels):
        shifted = shifter(stream, 2**level)
        high = high0 * stream + high1 * shifted
        stream = low0 * stream + low1 * shifted
        mixed = mixed + mix[level] * high
    return mixed + mix[levels] * stream


def plain(tokens, low_angle, high_taps, level_mix, w_value, w_gate, out_weight):
    rows = tokens.shape[0]
    channels = tokens.shape[1]
    ways = lax.axis_size(("seq", "sub"))
    total = rows * ways
    narrow = channels // ways
    place = lax.axis_index(("seq", "sub")) * narrow
    columns = lax.all_to_all(tokens.T, ("seq", "sub"), split_axis=0, concat_axis=1, tiled=True)
    angle = lax.dynamic_slice_in_dim(low_angle, place, narrow, 0)[:, None]
    high_pair = lax.dynamic_slice_in_dim(high_taps, place, narrow, 1)[:, :, None]
    mix = lax.dynamic_slice_in_dim(level_mix, place, narrow, 1)[:, :, None]

    def shifter(stream, reach):
        if reach >= total:
            return jnp.zeros_like(stream)
        return jnp.concatenate(
            [jnp.zeros((stream.shape[0], reach), F32), stream[:, : total - reach]], 1
        )

    mixed = run_levels(
        columns.astype(F32),
        shifter,
        jnp.cos(angle),
        jnp.sin(angle),
        high_pair[0],
        high_pair[1],
        mix,
    )
    filtered = jax.nn.gelu(mixed).astype(BF16)
    activated = lax.all_to_all(filtered, ("seq", "sub"), split_axis=1, concat_axis=0, tiled=True).T
    piece = lax.all_gather(activated, "chan", axis=1, tiled=True)
    value = jnp.dot(piece, w_value, preferred_element_type=F32)
    gate = jnp.dot(piece, w_gate, preferred_element_type=F32)
    hidden = (value * jax.nn.sigmoid(gate)).astype(BF16)
    projected = jnp.dot(
        lax.all_gather(hidden, "chan", axis=1, tiled=True),
        out_weight,
        preferred_element_type=F32,
    )
    return (projected + tokens.astype(F32)).astype(BF16)


def kernel(
    ways,
    tokens,
    low_angle,
    high_taps,
    level_mix,
    w_value,
    w_gate,
    out_weight,
    out,
    toks,
    cols,
    hist,
    near,
    coef,
    act,
    piece,
    hid,
    wbuf,
    obuf,
    rbuf,
    done,
    sums,
    local_sem,
    in_send,
    in_recv,
    w_send,
    wx_recv,
    wa_recv,
    wb_recv,
    wc_recv,
    act_send,
    act_recv,
    near_recv,
    res_send,
    res_recv,
    out_sem,
):
    rows, half = tokens.shape
    total = rows * ways
    levels = level_mix.shape[0] - 2
    subs = 2
    y = lax.axis_index("groups")
    z = lax.axis_index("seq")
    x = lax.axis_index("chan")
    u = lax.axis_index("sub")
    me = z * subs + u
    nx, ny, nu = 1 - x, 1 - y, 1 - u
    low = lax.rem(z, 2)
    nz = z + 1 - 2 * low
    part = rows // 2
    sizes = [part // 8 * e for e in EIGHTHS]
    starts = [sum(sizes[:q]) for q in range(len(sizes))]
    chunks = len(sizes)
    depth = wbuf.shape[2]
    ws = (w_value, w_gate, out_weight)

    barrier = pltpu.get_barrier_semaphore()
    for other in range(1, 2 * ways):
        them = lax.rem(me * 2 + x + other, 2 * ways)
        pl.semaphore_signal(
            barrier,
            inc=1,
            device_id={"seq": them // 4, "sub": lax.rem(them // 2, 2), "chan": lax.rem(them, 2)},
            device_id_type=MESH,
        )
    pl.semaphore_signal(barrier, inc=1, device_id={"groups": ny}, device_id_type=MESH)

    own_in = pltpu.make_async_copy(
        tokens.at[:, pl.ds(pl.multiple_of(me * LANES, LANES), LANES)],
        cols.at[pl.ds(pl.multiple_of(me * rows, rows), rows)],
        in_recv.at[me],
    )
    own_in.start()
    load = pltpu.make_async_copy(tokens, toks, local_sem.at[3])
    load.start()
    own_w = [pltpu.make_async_copy(ws[i], wbuf.at[i, x], local_sem.at[i]) for i in range(3)]
    for copy in own_w:
        copy.start()

    @pl.loop(0, total // STEP)
    def _(i):
        hist[pl.ds(pl.multiple_of(i * STEP, STEP), STEP)] = jnp.zeros((STEP, LANES), F32)

    near[...] = jnp.zeros_like(near)

    lanes = pl.ds(pl.multiple_of(me * LANES, LANES), LANES)
    angle = low_angle[0:1, lanes]
    low0, low1 = jnp.cos(angle), jnp.sin(angle)
    high0, high1 = high_taps[0:1, lanes], high_taps[1:2, lanes]
    mix = [level_mix[k : k + 1, lanes] for k in range(levels + 2)]
    slope = low0 / low1
    stay, step_up = high0 - high1 * slope, high1 / low1
    live = sum(2**k < total for k in range(levels))
    weights = [mix[levels + 1] + mix[0] * stay]
    scale = low0
    for k in range(1, levels + 1):
        weight = mix[k - 1] * step_up + (mix[k] * stay if k < levels else mix[k])
        weights.append(weight * scale)
        scale = scale * low0
    last = weights[live]
    for k in range(live + 1, levels + 1):
        last = last + weights[k]
    for k in range(live):
        coef[k : k + 1] = weights[k]
    coef[live : live + 1] = last
    coef[live + 1 : live + 2] = low1 / low0

    pl.semaphore_wait(barrier, 2 * ways)

    def in_copy(peer, source):
        columns = pl.ds(pl.multiple_of(peer * LANES, LANES), LANES)
        return pltpu.make_async_remote_copy(
            src_ref=tokens.at[:, columns],
            dst_ref=cols.at[pl.ds(pl.multiple_of(source * rows, rows), rows)],
            send_sem=in_send,
            recv_sem=in_recv.at[source],
            device_id={"seq": peer // subs, "sub": lax.rem(peer, subs)},
            device_id_type=MESH,
        )

    for other in range(1, ways):
        in_copy(lax.rem(me + other, ways), me).start()

    count = 3 * PIECES
    band = depth // PIECES
    quarter = band // 4
    spot = {"groups": y, "seq": low}
    beside = {"groups": {"groups": ny}, "seq": {"seq": nz}}

    def region(p, side, narrow=None):
        i, k = divmod(p, PIECES)
        base = k * band + (side * 2 + u) * quarter
        if narrow is None:
            return i, pl.ds(pl.multiple_of(base, quarter), quarter)
        fine = quarter // 2
        return i, pl.ds(pl.multiple_of(base + narrow * fine, fine), fine)

    def first_region(p):
        first, second = HOPS[p]
        return region(p, spot[second], spot[first] if first else None)

    def x_copy(p):
        i, at = first_region(p)
        return pltpu.make_async_remote_copy(
            src_ref=ws[i].at[at],
            dst_ref=wbuf.at[i, x, at],
            send_sem=w_send.at[0],
            recv_sem=wx_recv.at[p],
            device_id={"chan": nx},
            device_id_type=MESH,
        )

    def w_copy(i, at, sem, target):
        slot = wbuf.at[i, nx, at]
        return pltpu.make_async_remote_copy(
            src_ref=slot,
            dst_ref=slot,
            send_sem=w_send.at[1],
            recv_sem=sem,
            device_id=target,
            device_id_type=MESH,
        )

    def a_copy(p):
        return w_copy(*first_region(p), wa_recv.at[p], beside[HOPS[p][0]])

    def b_copy(p):
        second = HOPS[p][1]
        return w_copy(*region(p, spot[second]), wb_recv.at[p], beside[second])

    def c_copy(p, other):
        side = spot[HOPS[p][1]]
        return w_copy(*region(p, 1 - side if other else side), wc_recv.at[p], {"sub": nu})

    def forward(p):
        b_copy(p).start()
        c_copy(p, False).start()

    def arrive(p):
        x_copy(p).wait_recv()
        if HOPS[p][0]:
            a_copy(p).start()
        else:
            forward(p)
        if p + AHEAD < count:
            x_copy(p + AHEAD).start()

    def turn(p):
        a_copy(p).wait_recv()
        forward(p)

    def across(p):
        b_copy(p).wait_recv()
        c_copy(p, True).start()

    def relay(steps):
        for step in steps:
            for act_on, p in zip((arrive, turn, across), step):
                if p is not None:
                    act_on(p)

    for p in range(AHEAD):
        x_copy(p).start()

    relay(BEFORE)

    def act_copy(owner, h, q, source, source_x, near):
        start = pl.multiple_of(owner * rows + h * part + starts[q], 16)
        to = pl.ds(pl.multiple_of(source_x * half + source * LANES, LANES), LANES)
        return pltpu.make_async_remote_copy(
            src_ref=act.at[pl.ds(start, sizes[q])],
            dst_ref=piece.at[pl.ds(starts[q], sizes[q]), to],
            send_sem=act_send.at[q],
            recv_sem=near_recv if near and q >= WHOLE else act_recv.at[q],
            device_id={"seq": owner // subs, "sub": lax.rem(owner, subs), "chan": h},
            device_id_type=MESH,
        )

    def own_act(q):
        start = pl.multiple_of(me * rows + x * part + starts[q], 16)
        to = pl.ds(pl.multiple_of(x * half + me * LANES, LANES), LANES)
        return pltpu.make_async_copy(
            act.at[pl.ds(start, sizes[q])],
            piece.at[pl.ds(starts[q], sizes[q]), to],
            near_recv if q >= WHOLE else act_recv.at[q],
        )

    def send_act(owner, q, near):
        for h in range(2):
            if not near:
                act_copy(owner, h, q, me, x, False).start()
                continue
            mine_too = jnp.logical_and(owner == me, x == h)

            @pl.when(mine_too)
            def _():
                own_act(q).start()

            @pl.when(jnp.logical_not(mine_too))
            def _():
                act_copy(owner, h, q, me, x, True).start()

    side = me // (ways // 2)

    def send_far(q):
        @pl.loop(0, ways // 2)
        def _(other):
            spread = lax.rem(me + other, ways // 2)
            send_act((1 - side) * (ways // 2) + spread, q, False)

    def advance(at):
        s = cols[pl.ds(at, STEP)].astype(F32)
        tan = coef[live + 1 : live + 2]
        m = coef[0:1] * s
        for k in range(live):
            reach = 2**k
            if reach < 8:
                near[k, 8 : 8 + STEP] = s
                d = near[k, 8 - reach : 8 - reach + STEP]
                near[k, 0:8] = s[STEP - 8 :]
            elif reach < STEP:
                d = jnp.concatenate([hist[reach : 2 * reach], s[: STEP - reach]], 0)
                hist[reach : 2 * reach] = s[STEP - reach :]
            else:
                slot = pl.ds(pl.multiple_of(reach + lax.rem(at, reach), STEP), STEP)
                d = hist[slot]
                hist[slot] = s
            s = s + tan * d
            m = m + coef[k + 1 : k + 2] * s
        act[pl.ds(at, STEP)] = jax.nn.gelu(m).astype(BF16)

    left = z < 2

    @pl.loop(0, ways)
    def _(block):
        for a, b, steps in DURING:
            when = a if a == b else jnp.where(left, a, b)

            @pl.when(block == when)
            def _():
                relay(steps)

        @pl.when(block != me)
        def _():
            in_copy(block, block).wait_recv()

        @pl.when(block == me)
        def _():
            own_in.wait()

        @pl.loop(0, rows // STEP)
        def _(i):
            advance(pl.multiple_of(block * rows + i * STEP, STEP))

        @pl.when(block // (ways // 2) == side)
        def _():
            for q in range(EARLY):
                send_act(block, q, True)

        @pl.when(block // (ways // 2) != side)
        def _():
            for q in range(EARLY):
                send_act(block, q, False)

    for q in range(EARLY, DEEP):
        send_far(q)

    @pl.loop(0, ways // 2)
    def _(other):
        owner = side * (ways // 2) + lax.rem(me + other, ways // 2)
        for q in range(EARLY, chunks):
            send_act(owner, q, True)

    relay(AFTER)

    def wait_bytes(ref, sem):
        pltpu.make_async_copy(ref, ref, sem).wait()

    def weights_here(i):
        own_w[i].wait()
        for p in range(i * PIECES, (i + 1) * PIECES):
            wait_bytes(wbuf.at[i, nx, pl.ds(0, 2 * quarter)], wc_recv.at[p])

    tiles = half // TILE

    def result_copy(q, tile):
        at = pl.ds(starts[q], sizes[q])
        lanes = pl.ds(pl.multiple_of(tile * TILE, TILE), TILE)
        return pltpu.make_async_remote_copy(
            src_ref=obuf.at[at, lanes],
            dst_ref=rbuf.at[at, lanes],
            send_sem=res_send,
            recv_sem=res_recv.at[q],
            device_id={"chan": nx},
            device_id_type=MESH,
        )

    def out_copy(q, owner):
        at = pl.ds(pl.multiple_of(owner * part + starts[q], 16), sizes[q])
        return pltpu.make_async_copy(done.at[at], out.at[at], out_sem)

    def sided(i, h, at, lanes, which):
        span = half // 2
        total_dot = None
        for source_x in range(2):
            deep = pl.ds(pl.multiple_of(source_x * half + which * span, span), span)
            dot = jnp.dot(piece[at, deep], wbuf[i, h, deep, lanes], preferred_element_type=F32)
            total_dot = dot if total_dot is None else total_dot + dot
        return total_dot

    def prepare():
        wait_bytes(piece.at[starts[WHOLE] :, 0:half], near_recv)
        at = pl.ds(starts[WHOLE], part - starts[WHOLE])
        for h in range(2):

            @pl.loop(0, tiles)
            def _(tile):
                lanes = pl.ds(pl.multiple_of(tile * TILE, TILE), TILE)
                for i in range(2):
                    sums[i, h * tiles + tile] = sided(i, h, at, lanes, side)

    def widen(q):
        at = pl.ds(starts[q], sizes[q])
        wait_bytes(piece.at[at] if q < WHOLE else piece.at[at, 0:half], act_recv.at[q])
        if q + DEEP < chunks:
            send_far(q + DEEP)
        if q == 0:
            weights_here(0)
            weights_here(1)

        for h in range(2):

            @pl.loop(0, tiles)
            def _(tile):
                lanes = pl.ds(pl.multiple_of(tile * TILE, TILE), TILE)
                if q < WHOLE:
                    value = jnp.dot(piece[at], wbuf[0, h, :, lanes], preferred_element_type=F32)
                    gate = jnp.dot(piece[at], wbuf[1, h, :, lanes], preferred_element_type=F32)
                else:
                    rest = pl.ds(starts[q] - starts[WHOLE], sizes[q])
                    value = sums[0, h * tiles + tile, rest] + sided(0, h, at, lanes, 1 - side)
                    gate = sums[1, h * tiles + tile, rest] + sided(1, h, at, lanes, 1 - side)
                to = pl.ds(pl.multiple_of(h * half + tile * TILE, TILE), TILE)
                hid[0 : sizes[q], to] = (value * jax.nn.sigmoid(gate)).astype(BF16)

    def project(q):
        @pl.loop(0, tiles)
        def _(tile):
            lanes = pl.ds(pl.multiple_of(tile * TILE, TILE), TILE)
            obuf[starts[q] : starts[q] + sizes[q], lanes] = jnp.dot(
                hid[0 : sizes[q]], wbuf[2, nx, :, lanes], preferred_element_type=F32
            ).astype(BF16)
            result_copy(q, tile).start()

        at = pl.ds(pl.multiple_of(x * part + starts[q], 16), sizes[q])

        @pl.loop(0, tiles)
        def _(tile):
            lanes = pl.ds(pl.multiple_of(tile * TILE, TILE), TILE)
            projected = jnp.dot(hid[0 : sizes[q]], wbuf[2, x, :, lanes], preferred_element_type=F32)
            done[at, lanes] = (projected + toks[at, lanes].astype(F32)).astype(BF16)

        out_copy(q, x).start()

    def finish(q):
        wait_bytes(rbuf.at[pl.ds(starts[q], sizes[q])], res_recv.at[q])
        base = nx * part + starts[q]

        @pl.loop(0, sizes[q] // 16)
        def _(i):
            at = pl.ds(pl.multiple_of(base + i * 16, 16), 16)
            got = rbuf[pl.ds(pl.multiple_of(starts[q] + i * 16, 16), 16)].astype(F32)
            done[at] = (got + toks[at].astype(F32)).astype(BF16)

        out_copy(q, nx).start()

    for q in range(chunks):
        widen(q)
        if q == 0:
            load.wait()
            weights_here(2)
        project(q)
        if q == 0:
            prepare()
    wait_bytes(cols.at[pl.ds(0, (ways - 1) * rows)], in_send)
    for p in range(count):
        x_copy(p).wait_send()
        if HOPS[p][0]:
            a_copy(p).wait_send()
        b_copy(p).wait_send()
        c_copy(p, False).wait_send()
        c_copy(p, True).wait_send()
    for q in range(chunks):
        wait_bytes(act.at[pl.ds(0, (2 * ways - 1) * sizes[q])], act_send.at[q])
    for q in range(chunks):
        finish(q)
    wait_bytes(obuf, res_send)
    wait_bytes(done, out_sem)


def fused(tokens, low_angle, high_taps, level_mix, w_value, w_gate, out_weight):
    rows, half = tokens.shape
    depth = w_value.shape[0]
    ways = lax.axis_size(("seq", "sub"))
    total = rows * ways
    part = rows // 2
    chunk = part // 8 * max(EIGHTHS)
    chunks = len(EIGHTHS)
    vmem = pl.BlockSpec(memory_space=pltpu.VMEM)
    hbm = pl.BlockSpec(memory_space=pl.ANY)
    dma = pltpu.SemaphoreType.DMA
    return pl.pallas_call(
        functools.partial(kernel, ways),
        out_shape=jax.ShapeDtypeStruct((rows, half), BF16),
        in_specs=[hbm, vmem, vmem, vmem, hbm, hbm, hbm],
        out_specs=hbm,
        scratch_shapes=[
            pltpu.VMEM((rows, half), BF16),
            pltpu.VMEM((total, LANES), BF16),
            pltpu.VMEM((total, LANES), F32),
            pltpu.VMEM((3, STEP + 8, LANES), F32),
            pltpu.VMEM((level_mix.shape[0] + 7, LANES), F32),
            pltpu.VMEM((total, LANES), BF16),
            pltpu.VMEM((part, depth), BF16),
            pltpu.VMEM((chunk, depth), BF16),
            pltpu.VMEM((3, 2, depth, half), BF16),
            pltpu.VMEM((part, half), BF16),
            pltpu.VMEM((part, half), BF16),
            pltpu.VMEM((rows, half), BF16),
            pltpu.VMEM((2, 2 * half // TILE, part - part // 8 * sum(EIGHTHS[:WHOLE]), TILE), F32),
            dma((4,)),
            dma(()),
            dma((ways,)),
            dma((2,)),
            dma((3 * PIECES,)),
            dma((3 * PIECES,)),
            dma((3 * PIECES,)),
            dma((3 * PIECES,)),
            dma((chunks,)),
            dma((chunks,)),
            dma(()),
            dma(()),
            dma((chunks,)),
            dma(()),
        ],
        compiler_params=pltpu.CompilerParams(
            collective_id=0, has_side_effects=True, vmem_limit_bytes=50 * 1024 * 1024
        ),
        name="layer",
    )(tokens, low_angle[None], high_taps, level_mix, w_value, w_gate, out_weight)


def solution(mesh):
    shape = mesh.shape
    pair = shape["groups"] == 2 and shape["chan"] == 2 and shape["sub"] == 2 and shape["seq"] == 4
    ways = shape["seq"] * shape["sub"]

    def shards(tokens, *rest):
        rows, half = tokens.shape
        fits = half == ways * LANES and rows % STEP == 0 and rows % 256 == 0 and half % TILE == 0
        whole = rest[3].shape[0] == 2 * half and rows * ways * LANES <= 1 << 20
        body = fused if pair and fits and whole else plain
        return body(tokens, *rest)

    return jax.shard_map(
        shards,
        mesh=mesh,
        in_specs=(
            P(("groups", "seq", "sub"), "chan"),
            P("chan"),
            P(None, "chan"),
            P(None, "chan"),
            P(None, "chan"),
            P(None, "chan"),
            P(None, "chan"),
        ),
        out_specs=P(("groups", "seq", "sub"), "chan"),
        check_vma=False,
    )
```

```python
import functools

import jax
import jax.numpy as jnp
from jax import lax
from jax.experimental import pallas as pl
from jax.experimental.pallas import tpu as pltpu
from jax.sharding import PartitionSpec as P

MESH = pl.DeviceIdType.MESH
F32 = jnp.float32
BF16 = jnp.bfloat16
LANES = 128
STEP = 128
TILE = 512
PIECES = 4
OVER_Y = (None, "groups")
OVER_Z = (None, "seq")
ZY = ("seq", "groups")
YZ = ("groups", "seq")
HOPS = (YZ,) * 4 + (OVER_Y,) * 8
N = None
BEFORE = ((0, N, N), (1, 0, N), (2, 1, N), (3, 2, N), (4, 3, N), (5, N, 4), (6, N, 5))
DURING = ((1, 0, ((7, N, 6),)), (3, 0, ((8, N, 7),)), (6, 4, ((9, N, 8),)))
AFTER = ((10, N, 9), (N, N, 0), (N, N, 1), (N, N, 2), (N, N, 3), (11, N, 10), (N, N, 11))
SLICES = 8
EARLY = 2
DEEP = 5
WHOLE = 2
AHEAD = 4
EIGHTHS = (2, 2, 2, 2)


def run_levels(stream, shifter, low0, low1, high0, high1, mix):
    levels = mix.shape[0] - 2
    mixed = mix[levels + 1] * stream
    for level in range(levels):
        shifted = shifter(stream, 2**level)
        high = high0 * stream + high1 * shifted
        stream = low0 * stream + low1 * shifted
        mixed = mixed + mix[level] * high
    return mixed + mix[levels] * stream


def plain(tokens, low_angle, high_taps, level_mix, w_value, w_gate, out_weight):
    rows = tokens.shape[0]
    channels = tokens.shape[1]
    ways = lax.axis_size(("seq", "sub"))
    total = rows * ways
    narrow = channels // ways
    place = lax.axis_index(("seq", "sub")) * narrow
    columns = lax.all_to_all(tokens.T, ("seq", "sub"), split_axis=0, concat_axis=1, tiled=True)
    angle = lax.dynamic_slice_in_dim(low_angle, place, narrow, 0)[:, None]
    high_pair = lax.dynamic_slice_in_dim(high_taps, place, narrow, 1)[:, :, None]
    mix = lax.dynamic_slice_in_dim(level_mix, place, narrow, 1)[:, :, None]

    def shifter(stream, reach):
        if reach >= total:
            return jnp.zeros_like(stream)
        return jnp.concatenate(
            [jnp.zeros((stream.shape[0], reach), F32), stream[:, : total - reach]], 1
        )

    mixed = run_levels(
        columns.astype(F32),
        shifter,
        jnp.cos(angle),
        jnp.sin(angle),
        high_pair[0],
        high_pair[1],
        mix,
    )
    filtered = jax.nn.gelu(mixed).astype(BF16)
    activated = lax.all_to_all(filtered, ("seq", "sub"), split_axis=1, concat_axis=0, tiled=True).T
    piece = lax.all_gather(activated, "chan", axis=1, tiled=True)
    value = jnp.dot(piece, w_value, preferred_element_type=F32)
    gate = jnp.dot(piece, w_gate, preferred_element_type=F32)
    hidden = (value * jax.nn.sigmoid(gate)).astype(BF16)
    projected = jnp.dot(
        lax.all_gather(hidden, "chan", axis=1, tiled=True),
        out_weight,
        preferred_element_type=F32,
    )
    return (projected + tokens.astype(F32)).astype(BF16)


def kernel(
    ways,
    tokens,
    low_angle,
    high_taps,
    level_mix,
    w_value,
    w_gate,
    out_weight,
    out,
    toks,
    cols,
    hist,
    near,
    coef,
    act,
    piece,
    hid,
    wbuf,
    obuf,
    rbuf,
    done,
    sums,
    local_sem,
    in_send,
    in_recv,
    w_send,
    wx_recv,
    wa_recv,
    wb_recv,
    wc_recv,
    act_send,
    act_recv,
    near_recv,
    res_send,
    res_recv,
    out_sem,
):
    rows, half = tokens.shape
    total = rows * ways
    levels = level_mix.shape[0] - 2
    subs = 2
    y = lax.axis_index("groups")
    z = lax.axis_index("seq")
    x = lax.axis_index("chan")
    u = lax.axis_index("sub")
    me = z * subs + u
    nx, ny, nu = 1 - x, 1 - y, 1 - u
    low = lax.rem(z, 2)
    nz = z + 1 - 2 * low
    part = rows // 2
    sizes = [part // 8 * e for e in EIGHTHS]
    starts = [sum(sizes[:q]) for q in range(len(sizes))]
    chunks = len(sizes)
    depth = wbuf.shape[2]
    ws = (w_value, w_gate, out_weight)

    barrier = pltpu.get_barrier_semaphore()
    for other in range(1, 2 * ways):
        them = lax.rem(me * 2 + x + other, 2 * ways)
        pl.semaphore_signal(
            barrier,
            inc=1,
            device_id={"seq": them // 4, "sub": lax.rem(them // 2, 2), "chan": lax.rem(them, 2)},
            device_id_type=MESH,
        )
    pl.semaphore_signal(barrier, inc=1, device_id={"groups": ny}, device_id_type=MESH)

    own_in = pltpu.make_async_copy(
        tokens.at[:, pl.ds(pl.multiple_of(me * LANES, LANES), LANES)],
        cols.at[pl.ds(pl.multiple_of(me * rows, rows), rows)],
        in_recv.at[me],
    )
    own_in.start()
    load = pltpu.make_async_copy(tokens, toks, local_sem.at[3])
    load.start()
    own_w = [pltpu.make_async_copy(ws[i], wbuf.at[i, x], local_sem.at[i]) for i in range(3)]
    for copy in own_w:
        copy.start()

    @pl.loop(0, total // STEP)
    def _(i):
        hist[pl.ds(pl.multiple_of(i * STEP, STEP), STEP)] = jnp.zeros((STEP, LANES), F32)

    near[...] = jnp.zeros_like(near)

    lanes = pl.ds(pl.multiple_of(me * LANES, LANES), LANES)
    angle = low_angle[0:1, lanes]
    low0, low1 = jnp.cos(angle), jnp.sin(angle)
    high0, high1 = high_taps[0:1, lanes], high_taps[1:2, lanes]
    mix = [level_mix[k : k + 1, lanes] for k in range(levels + 2)]
    slope = low0 / low1
    stay, step_up = high0 - high1 * slope, high1 / low1
    live = sum(2**k < total for k in range(levels))
    weights = [mix[levels + 1] + mix[0] * stay]
    scale = low0
    for k in range(1, levels + 1):
        weight = mix[k - 1] * step_up + (mix[k] * stay if k < levels else mix[k])
        weights.append(weight * scale)
        scale = scale * low0
    last = weights[live]
    for k in range(live + 1, levels + 1):
        last = last + weights[k]
    for k in range(live):
        coef[k : k + 1] = weights[k]
    coef[live : live + 1] = last
    coef[live + 1 : live + 2] = low1 / low0

    pl.semaphore_wait(barrier, 2 * ways)

    def in_copy(peer, source):
        columns = pl.ds(pl.multiple_of(peer * LANES, LANES), LANES)
        return pltpu.make_async_remote_copy(
            src_ref=tokens.at[:, columns],
            dst_ref=cols.at[pl.ds(pl.multiple_of(source * rows, rows), rows)],
            send_sem=in_send,
            recv_sem=in_recv.at[source],
            device_id={"seq": peer // subs, "sub": lax.rem(peer, subs)},
            device_id_type=MESH,
        )

    for other in sorted(range(1, ways), key=lambda other: abs(other - ways // 2)):
        in_copy(lax.rem(me + other, ways), me).start()

    count = 3 * PIECES
    band = depth // PIECES
    quarter = band // 4
    spot = {"groups": y, "seq": low}
    beside = {"groups": {"groups": ny}, "seq": {"seq": nz}}

    def region(p, side, narrow=None):
        i, k = divmod(p, PIECES)
        base = k * band + (side * 2 + u) * quarter
        if narrow is None:
            return i, pl.ds(pl.multiple_of(base, quarter), quarter)
        fine = quarter // 2
        return i, pl.ds(pl.multiple_of(base + narrow * fine, fine), fine)

    def first_region(p):
        first, second = HOPS[p]
        return region(p, spot[second], spot[first] if first else None)

    def x_copy(p):
        i, at = first_region(p)
        return pltpu.make_async_remote_copy(
            src_ref=ws[i].at[at],
            dst_ref=wbuf.at[i, x, at],
            send_sem=w_send.at[0],
            recv_sem=wx_recv.at[p],
            device_id={"chan": nx},
            device_id_type=MESH,
        )

    def w_copy(i, at, sem, target):
        slot = wbuf.at[i, nx, at]
        return pltpu.make_async_remote_copy(
            src_ref=slot,
            dst_ref=slot,
            send_sem=w_send.at[1],
            recv_sem=sem,
            device_id=target,
            device_id_type=MESH,
        )

    def a_copy(p):
        return w_copy(*first_region(p), wa_recv.at[p], beside[HOPS[p][0]])

    def b_copy(p):
        second = HOPS[p][1]
        return w_copy(*region(p, spot[second]), wb_recv.at[p], beside[second])

    def c_copy(p, other):
        side = spot[HOPS[p][1]]
        return w_copy(*region(p, 1 - side if other else side), wc_recv.at[p], {"sub": nu})

    def forward(p):
        b_copy(p).start()
        c_copy(p, False).start()

    def arrive(p):
        x_copy(p).wait_recv()
        if HOPS[p][0]:
            a_copy(p).start()
        else:
            forward(p)
        if p + AHEAD < count:
            x_copy(p + AHEAD).start()

    def turn(p):
        a_copy(p).wait_recv()
        forward(p)

    def across(p):
        b_copy(p).wait_recv()
        c_copy(p, True).start()

    def relay(steps):
        for step in steps:
            for act_on, p in zip((arrive, turn, across), step):
                if p is not None:
                    act_on(p)

    for p in range(AHEAD):
        x_copy(p).start()

    relay(BEFORE)

    def act_copy(owner, h, first, length, source, source_x, sem):
        start = pl.multiple_of(owner * rows + h * part + first, 16)
        to = pl.ds(pl.multiple_of(source_x * half + source * LANES, LANES), LANES)
        return pltpu.make_async_remote_copy(
            src_ref=act.at[pl.ds(start, length)],
            dst_ref=piece.at[pl.ds(first, length), to],
            send_sem=act_send,
            recv_sem=sem,
            device_id={"seq": owner // subs, "sub": lax.rem(owner, subs), "chan": h},
            device_id_type=MESH,
        )

    def near_sem(q):
        return near_recv.at[min(q, WHOLE)]

    def own_act(q):
        start = pl.multiple_of(me * rows + x * part + starts[q], 16)
        to = pl.ds(pl.multiple_of(x * half + me * LANES, LANES), LANES)
        return pltpu.make_async_copy(
            act.at[pl.ds(start, sizes[q])], piece.at[pl.ds(starts[q], sizes[q]), to], near_sem(q)
        )

    def send_near(owner, q):
        for h in range(2):
            mine_too = jnp.logical_and(owner == me, x == h)

            @pl.when(mine_too)
            def _():
                own_act(q).start()

            @pl.when(jnp.logical_not(mine_too))
            def _():
                act_copy(owner, h, starts[q], sizes[q], me, x, near_sem(q)).start()

    side = me // (ways // 2)
    short = part // SLICES

    def send_slice(owner, c):
        for h in range(2):
            act_copy(owner, h, c * short, short, me, x, act_recv.at[c]).start()

    def send_far(c):
        @pl.loop(0, ways // 2)
        def _(other):
            spread = lax.rem(me + other, ways // 2)
            send_slice((1 - side) * (ways // 2) + spread, c)

    def advance(at):
        s = cols[pl.ds(at, STEP)].astype(F32)
        tan = coef[live + 1 : live + 2]
        m = coef[0:1] * s
        for k in range(live):
            reach = 2**k
            if reach < 8:
                near[k, 8 : 8 + STEP] = s
                d = near[k, 8 - reach : 8 - reach + STEP]
                near[k, 0:8] = s[STEP - 8 :]
            elif reach < STEP:
                d = jnp.concatenate([hist[reach : 2 * reach], s[: STEP - reach]], 0)
                hist[reach : 2 * reach] = s[STEP - reach :]
            else:
                slot = pl.ds(pl.multiple_of(reach + lax.rem(at, reach), STEP), STEP)
                d = hist[slot]
                hist[slot] = s
            s = s + tan * d
            m = m + coef[k + 1 : k + 2] * s
        act[pl.ds(at, STEP)] = jax.nn.gelu(m).astype(BF16)

    left = z < 2

    @pl.loop(0, ways)
    def _(block):
        for a, b, steps in DURING:
            when = a if a == b else jnp.where(left, a, b)

            @pl.when(block == when)
            def _():
                relay(steps)

        @pl.when(block != me)
        def _():
            in_copy(block, block).wait_recv()

        @pl.when(block == me)
        def _():
            own_in.wait()

        @pl.loop(0, rows // STEP)
        def _(i):
            advance(pl.multiple_of(block * rows + i * STEP, STEP))

        @pl.when(block // (ways // 2) == side)
        def _():
            send_near(block, 0)

        @pl.when(block // (ways // 2) != side)
        def _():
            for c in range(EARLY):
                send_slice(block, c)

    for c in range(EARLY, DEEP):
        send_far(c)

    @pl.loop(0, ways // 2)
    def _(other):
        owner = side * (ways // 2) + lax.rem(me + other, ways // 2)
        for q in range(1, chunks):
            send_near(owner, q)

    relay(AFTER)

    def wait_bytes(ref, sem):
        pltpu.make_async_copy(ref, ref, sem).wait()

    def weights_here(i):
        own_w[i].wait()
        for p in range(i * PIECES, (i + 1) * PIECES):
            wait_bytes(wbuf.at[i, nx, pl.ds(0, 2 * quarter)], wc_recv.at[p])

    tiles = half // TILE

    def result_copy(q, tile):
        at = pl.ds(starts[q], sizes[q])
        lanes = pl.ds(pl.multiple_of(tile * TILE, TILE), TILE)
        return pltpu.make_async_remote_copy(
            src_ref=obuf.at[at, lanes],
            dst_ref=rbuf.at[at, lanes],
            send_sem=res_send,
            recv_sem=res_recv.at[q],
            device_id={"chan": nx},
            device_id_type=MESH,
        )

    def out_copy(q, owner):
        at = pl.ds(pl.multiple_of(owner * part + starts[q], 16), sizes[q])
        return pltpu.make_async_copy(done.at[at], out.at[at], out_sem)

    def sided(i, h, at, lanes, which):
        span = half // 2
        total_dot = None
        for source_x in range(2):
            deep = pl.ds(pl.multiple_of(source_x * half + which * span, span), span)
            dot = jnp.dot(piece[at, deep], wbuf[i, h, deep, lanes], preferred_element_type=F32)
            total_dot = dot if total_dot is None else total_dot + dot
        return total_dot

    def prepare():
        wait_bytes(piece.at[starts[WHOLE] :, 0:half], near_sem(WHOLE))
        at = pl.ds(starts[WHOLE], part - starts[WHOLE])
        for h in range(2):

            @pl.loop(0, tiles)
            def _(tile):
                lanes = pl.ds(pl.multiple_of(tile * TILE, TILE), TILE)
                for i in range(2):
                    sums[i, h * tiles + tile] = sided(i, h, at, lanes, side)

    def widen(q):
        at = pl.ds(starts[q], sizes[q])
        for c in range(SLICES):
            if starts[q] <= c * short < starts[q] + sizes[q]:
                wait_bytes(piece.at[0:short, 0:half], act_recv.at[c])
                if c + DEEP < SLICES:
                    send_far(c + DEEP)
        if q < WHOLE:
            wait_bytes(piece.at[at, 0:half], near_sem(q))
        if q == 0:
            weights_here(0)
            weights_here(1)

        for h in range(2):

            @pl.loop(0, tiles)
            def _(tile):
                lanes = pl.ds(pl.multiple_of(tile * TILE, TILE), TILE)
                if q < WHOLE:
                    value = jnp.dot(piece[at], wbuf[0, h, :, lanes], preferred_element_type=F32)
                    gate = jnp.dot(piece[at], wbuf[1, h, :, lanes], preferred_element_type=F32)
                else:
                    rest = pl.ds(starts[q] - starts[WHOLE], sizes[q])
                    value = sums[0, h * tiles + tile, rest] + sided(0, h, at, lanes, 1 - side)
                    gate = sums[1, h * tiles + tile, rest] + sided(1, h, at, lanes, 1 - side)
                to = pl.ds(pl.multiple_of(h * half + tile * TILE, TILE), TILE)
                hid[0 : sizes[q], to] = (value * jax.nn.sigmoid(gate)).astype(BF16)

    def project(q):
        @pl.loop(0, tiles)
        def _(tile):
            lanes = pl.ds(pl.multiple_of(tile * TILE, TILE), TILE)
            obuf[starts[q] : starts[q] + sizes[q], lanes] = jnp.dot(
                hid[0 : sizes[q]], wbuf[2, nx, :, lanes], preferred_element_type=F32
            ).astype(BF16)
            result_copy(q, tile).start()

        at = pl.ds(pl.multiple_of(x * part + starts[q], 16), sizes[q])

        @pl.loop(0, tiles)
        def _(tile):
            lanes = pl.ds(pl.multiple_of(tile * TILE, TILE), TILE)
            projected = jnp.dot(hid[0 : sizes[q]], wbuf[2, x, :, lanes], preferred_element_type=F32)
            done[at, lanes] = (projected + toks[at, lanes].astype(F32)).astype(BF16)

        out_copy(q, x).start()

    def finish(q):
        wait_bytes(rbuf.at[pl.ds(starts[q], sizes[q])], res_recv.at[q])
        base = nx * part + starts[q]

        @pl.loop(0, sizes[q] // 16)
        def _(i):
            at = pl.ds(pl.multiple_of(base + i * 16, 16), 16)
            got = rbuf[pl.ds(pl.multiple_of(starts[q] + i * 16, 16), 16)].astype(F32)
            done[at] = (got + toks[at].astype(F32)).astype(BF16)

        out_copy(q, nx).start()

    for q in range(chunks):
        widen(q)
        if q == 0:
            load.wait()
            weights_here(2)
        project(q)
        if q == WHOLE - 1:
            prepare()
    wait_bytes(cols.at[pl.ds(0, (ways - 1) * rows)], in_send)
    for p in range(count):
        x_copy(p).wait_send()
        if HOPS[p][0]:
            a_copy(p).wait_send()
        b_copy(p).wait_send()
        c_copy(p, False).wait_send()
        c_copy(p, True).wait_send()
    wait_bytes(act.at[pl.ds(0, (2 * ways - 1) * part)], act_send)
    for q in range(chunks):
        finish(q)
    wait_bytes(obuf, res_send)
    wait_bytes(done, out_sem)


def fused(tokens, low_angle, high_taps, level_mix, w_value, w_gate, out_weight):
    rows, half = tokens.shape
    depth = w_value.shape[0]
    ways = lax.axis_size(("seq", "sub"))
    total = rows * ways
    part = rows // 2
    chunk = part // 8 * max(EIGHTHS)
    chunks = len(EIGHTHS)
    vmem = pl.BlockSpec(memory_space=pltpu.VMEM)
    hbm = pl.BlockSpec(memory_space=pl.ANY)
    dma = pltpu.SemaphoreType.DMA
    return pl.pallas_call(
        functools.partial(kernel, ways),
        out_shape=jax.ShapeDtypeStruct((rows, half), BF16),
        in_specs=[hbm, vmem, vmem, vmem, hbm, hbm, hbm],
        out_specs=hbm,
        scratch_shapes=[
            pltpu.VMEM((rows, half), BF16),
            pltpu.VMEM((total, LANES), BF16),
            pltpu.VMEM((total, LANES), F32),
            pltpu.VMEM((3, STEP + 8, LANES), F32),
            pltpu.VMEM((level_mix.shape[0] + 7, LANES), F32),
            pltpu.VMEM((total, LANES), BF16),
            pltpu.VMEM((part, depth), BF16),
            pltpu.VMEM((chunk, depth), BF16),
            pltpu.VMEM((3, 2, depth, half), BF16),
            pltpu.VMEM((part, half), BF16),
            pltpu.VMEM((part, half), BF16),
            pltpu.VMEM((rows, half), BF16),
            pltpu.VMEM((2, 2 * half // TILE, part - part // 8 * sum(EIGHTHS[:WHOLE]), TILE), F32),
            dma((4,)),
            dma(()),
            dma((ways,)),
            dma((2,)),
            dma((3 * PIECES,)),
            dma((3 * PIECES,)),
            dma((3 * PIECES,)),
            dma((3 * PIECES,)),
            dma(()),
            dma((SLICES,)),
            dma((WHOLE + 1,)),
            dma(()),
            dma((chunks,)),
            dma(()),
        ],
        compiler_params=pltpu.CompilerParams(
            collective_id=0, has_side_effects=True, vmem_limit_bytes=50 * 1024 * 1024
        ),
        name="layer",
    )(tokens, low_angle[None], high_taps, level_mix, w_value, w_gate, out_weight)


def solution(mesh):
    shape = mesh.shape
    pair = shape["groups"] == 2 and shape["chan"] == 2 and shape["sub"] == 2 and shape["seq"] == 4
    ways = shape["seq"] * shape["sub"]

    def shards(tokens, *rest):
        rows, half = tokens.shape
        fits = half == ways * LANES and rows % STEP == 0 and rows % 256 == 0 and half % TILE == 0
        whole = rest[3].shape[0] == 2 * half and rows * ways * LANES <= 1 << 20
        body = fused if pair and fits and whole else plain
        return body(tokens, *rest)

    return jax.shard_map(
        shards,
        mesh=mesh,
        in_specs=(
            P(("groups", "seq", "sub"), "chan"),
            P("chan"),
            P(None, "chan"),
            P(None, "chan"),
            P(None, "chan"),
            P(None, "chan"),
            P(None, "chan"),
        ),
        out_specs=P(("groups", "seq", "sub"), "chan"),
        check_vma=False,
    )
```

```python
import functools

import jax
import jax.numpy as jnp
from jax import lax
from jax.experimental import pallas as pl
from jax.experimental.pallas import tpu as pltpu
from jax.sharding import PartitionSpec as P

MESH = pl.DeviceIdType.MESH
F32 = jnp.float32
BF16 = jnp.bfloat16
LANES = 128
STEP = 128
TILE = 512
PIECES = 4
OVER_Y = (None, "groups")
OVER_Z = (None, "seq")
ZY = ("seq", "groups")
YZ = ("groups", "seq")
HOPS = (YZ,) * 4 + (OVER_Y,) * 8
N = None
BEFORE = ((0, N, N), (1, 0, N), (2, 1, N), (3, 2, N), (4, 3, N), (5, N, 4), (6, N, 5))
DURING = ((1, 0, ((7, N, 6),)), (3, 0, ((8, N, 7),)), (6, 4, ((9, N, 8),)))
AFTER = ((10, N, 9), (N, N, 0), (N, N, 1), (N, N, 2), (N, N, 3), (11, N, 10), (N, N, 11))
SLICES = 8
EARLY = 2
DEEP = 5
WHOLE = 2
AHEAD = 6
EIGHTHS = (2, 2, 2, 2)


def run_levels(stream, shifter, low0, low1, high0, high1, mix):
    levels = mix.shape[0] - 2
    mixed = mix[levels + 1] * stream
    for level in range(levels):
        shifted = shifter(stream, 2**level)
        high = high0 * stream + high1 * shifted
        stream = low0 * stream + low1 * shifted
        mixed = mixed + mix[level] * high
    return mixed + mix[levels] * stream


def plain(tokens, low_angle, high_taps, level_mix, w_value, w_gate, out_weight):
    rows = tokens.shape[0]
    channels = tokens.shape[1]
    ways = lax.axis_size(("seq", "sub"))
    total = rows * ways
    narrow = channels // ways
    place = lax.axis_index(("seq", "sub")) * narrow
    columns = lax.all_to_all(tokens.T, ("seq", "sub"), split_axis=0, concat_axis=1, tiled=True)
    angle = lax.dynamic_slice_in_dim(low_angle, place, narrow, 0)[:, None]
    high_pair = lax.dynamic_slice_in_dim(high_taps, place, narrow, 1)[:, :, None]
    mix = lax.dynamic_slice_in_dim(level_mix, place, narrow, 1)[:, :, None]

    def shifter(stream, reach):
        if reach >= total:
            return jnp.zeros_like(stream)
        return jnp.concatenate(
            [jnp.zeros((stream.shape[0], reach), F32), stream[:, : total - reach]], 1
        )

    mixed = run_levels(
        columns.astype(F32),
        shifter,
        jnp.cos(angle),
        jnp.sin(angle),
        high_pair[0],
        high_pair[1],
        mix,
    )
    filtered = jax.nn.gelu(mixed).astype(BF16)
    activated = lax.all_to_all(filtered, ("seq", "sub"), split_axis=1, concat_axis=0, tiled=True).T
    piece = lax.all_gather(activated, "chan", axis=1, tiled=True)
    value = jnp.dot(piece, w_value, preferred_element_type=F32)
    gate = jnp.dot(piece, w_gate, preferred_element_type=F32)
    hidden = (value * jax.nn.sigmoid(gate)).astype(BF16)
    projected = jnp.dot(
        lax.all_gather(hidden, "chan", axis=1, tiled=True),
        out_weight,
        preferred_element_type=F32,
    )
    return (projected + tokens.astype(F32)).astype(BF16)


def kernel(
    ways,
    tokens,
    low_angle,
    high_taps,
    level_mix,
    w_value,
    w_gate,
    out_weight,
    out,
    toks,
    cols,
    hist,
    near,
    coef,
    act,
    piece,
    hid,
    wbuf,
    obuf,
    rbuf,
    done,
    sums,
    local_sem,
    in_send,
    in_recv,
    w_send,
    wx_recv,
    wa_recv,
    wb_recv,
    wc_recv,
    act_send,
    act_recv,
    near_recv,
    res_send,
    res_recv,
    out_sem,
):
    rows, half = tokens.shape
    total = rows * ways
    levels = level_mix.shape[0] - 2
    subs = 2
    y = lax.axis_index("groups")
    z = lax.axis_index("seq")
    x = lax.axis_index("chan")
    u = lax.axis_index("sub")
    me = z * subs + u
    nx, ny, nu = 1 - x, 1 - y, 1 - u
    low = lax.rem(z, 2)
    nz = z + 1 - 2 * low
    part = rows // 2
    sizes = [part // 8 * e for e in EIGHTHS]
    starts = [sum(sizes[:q]) for q in range(len(sizes))]
    chunks = len(sizes)
    depth = wbuf.shape[2]
    ws = (w_value, w_gate, out_weight)

    barrier = pltpu.get_barrier_semaphore()
    for other in range(1, 2 * ways):
        them = lax.rem(me * 2 + x + other, 2 * ways)
        pl.semaphore_signal(
            barrier,
            inc=1,
            device_id={"seq": them // 4, "sub": lax.rem(them // 2, 2), "chan": lax.rem(them, 2)},
            device_id_type=MESH,
        )
    pl.semaphore_signal(barrier, inc=1, device_id={"groups": ny}, device_id_type=MESH)

    own_in = pltpu.make_async_copy(
        tokens.at[:, pl.ds(pl.multiple_of(me * LANES, LANES), LANES)],
        cols.at[pl.ds(pl.multiple_of(me * rows, rows), rows)],
        in_recv.at[me],
    )
    own_in.start()
    load = pltpu.make_async_copy(tokens, toks, local_sem.at[3])
    load.start()
    own_w = [pltpu.make_async_copy(ws[i], wbuf.at[i, x], local_sem.at[i]) for i in range(3)]
    for copy in own_w:
        copy.start()

    @pl.loop(0, total // STEP)
    def _(i):
        hist[pl.ds(pl.multiple_of(i * STEP, STEP), STEP)] = jnp.zeros((STEP, LANES), F32)

    near[...] = jnp.zeros_like(near)

    lanes = pl.ds(pl.multiple_of(me * LANES, LANES), LANES)
    angle = low_angle[0:1, lanes]
    low0, low1 = jnp.cos(angle), jnp.sin(angle)
    high0, high1 = high_taps[0:1, lanes], high_taps[1:2, lanes]
    mix = [level_mix[k : k + 1, lanes] for k in range(levels + 2)]
    slope = low0 / low1
    stay, step_up = high0 - high1 * slope, high1 / low1
    live = sum(2**k < total for k in range(levels))
    weights = [mix[levels + 1] + mix[0] * stay]
    scale = low0
    for k in range(1, levels + 1):
        weight = mix[k - 1] * step_up + (mix[k] * stay if k < levels else mix[k])
        weights.append(weight * scale)
        scale = scale * low0
    last = weights[live]
    for k in range(live + 1, levels + 1):
        last = last + weights[k]
    for k in range(live):
        coef[k : k + 1] = weights[k]
    coef[live : live + 1] = last
    coef[live + 1 : live + 2] = low1 / low0

    pl.semaphore_wait(barrier, 2 * ways)

    def in_copy(peer, source):
        columns = pl.ds(pl.multiple_of(peer * LANES, LANES), LANES)
        return pltpu.make_async_remote_copy(
            src_ref=tokens.at[:, columns],
            dst_ref=cols.at[pl.ds(pl.multiple_of(source * rows, rows), rows)],
            send_sem=in_send,
            recv_sem=in_recv.at[source],
            device_id={"seq": peer // subs, "sub": lax.rem(peer, subs)},
            device_id_type=MESH,
        )

    for other in sorted(range(1, ways), key=lambda other: abs(other - ways // 2)):
        in_copy(lax.rem(me + other, ways), me).start()

    count = 3 * PIECES
    band = depth // PIECES
    quarter = band // 4
    spot = {"groups": y, "seq": low}
    beside = {"groups": {"groups": ny}, "seq": {"seq": nz}}

    def region(p, side, narrow=None):
        i, k = divmod(p, PIECES)
        base = k * band + (side * 2 + u) * quarter
        if narrow is None:
            return i, pl.ds(pl.multiple_of(base, quarter), quarter)
        fine = quarter // 2
        return i, pl.ds(pl.multiple_of(base + narrow * fine, fine), fine)

    def first_region(p):
        first, second = HOPS[p]
        return region(p, spot[second], spot[first] if first else None)

    def x_copy(p):
        i, at = first_region(p)
        return pltpu.make_async_remote_copy(
            src_ref=ws[i].at[at],
            dst_ref=wbuf.at[i, x, at],
            send_sem=w_send.at[0],
            recv_sem=wx_recv.at[p],
            device_id={"chan": nx},
            device_id_type=MESH,
        )

    def w_copy(i, at, sem, target):
        slot = wbuf.at[i, nx, at]
        return pltpu.make_async_remote_copy(
            src_ref=slot,
            dst_ref=slot,
            send_sem=w_send.at[1],
            recv_sem=sem,
            device_id=target,
            device_id_type=MESH,
        )

    def a_copy(p):
        return w_copy(*first_region(p), wa_recv.at[p], beside[HOPS[p][0]])

    def b_copy(p):
        second = HOPS[p][1]
        return w_copy(*region(p, spot[second]), wb_recv.at[p], beside[second])

    def c_copy(p, other):
        side = spot[HOPS[p][1]]
        return w_copy(*region(p, 1 - side if other else side), wc_recv.at[p], {"sub": nu})

    def forward(p):
        b_copy(p).start()
        c_copy(p, False).start()

    def arrive(p):
        x_copy(p).wait_recv()
        if HOPS[p][0]:
            a_copy(p).start()
        else:
            forward(p)
        if p + AHEAD < count:
            x_copy(p + AHEAD).start()

    def turn(p):
        a_copy(p).wait_recv()
        forward(p)

    def across(p):
        b_copy(p).wait_recv()
        c_copy(p, True).start()

    def relay(steps):
        for step in steps:
            for act_on, p in zip((arrive, turn, across), step):
                if p is not None:
                    act_on(p)

    for p in range(AHEAD):
        x_copy(p).start()

    relay(BEFORE)

    def act_copy(owner, h, first, length, source, source_x, sem):
        start = pl.multiple_of(owner * rows + h * part + first, 16)
        to = pl.ds(pl.multiple_of(source_x * half + source * LANES, LANES), LANES)
        return pltpu.make_async_remote_copy(
            src_ref=act.at[pl.ds(start, length)],
            dst_ref=piece.at[pl.ds(first, length), to],
            send_sem=act_send,
            recv_sem=sem,
            device_id={"seq": owner // subs, "sub": lax.rem(owner, subs), "chan": h},
            device_id_type=MESH,
        )

    def near_sem(q):
        return near_recv.at[min(q, WHOLE)]

    def own_act(q):
        start = pl.multiple_of(me * rows + x * part + starts[q], 16)
        to = pl.ds(pl.multiple_of(x * half + me * LANES, LANES), LANES)
        return pltpu.make_async_copy(
            act.at[pl.ds(start, sizes[q])], piece.at[pl.ds(starts[q], sizes[q]), to], near_sem(q)
        )

    def send_near(owner, q):
        for h in range(2):
            mine_too = jnp.logical_and(owner == me, x == h)

            @pl.when(mine_too)
            def _():
                own_act(q).start()

            @pl.when(jnp.logical_not(mine_too))
            def _():
                act_copy(owner, h, starts[q], sizes[q], me, x, near_sem(q)).start()

    side = me // (ways // 2)
    short = part // SLICES

    def send_slice(owner, c):
        for h in range(2):
            act_copy(owner, h, c * short, short, me, x, act_recv.at[c]).start()

    def send_far(c):
        @pl.loop(0, ways // 2)
        def _(other):
            spread = lax.rem(me + other, ways // 2)
            send_slice((1 - side) * (ways // 2) + spread, c)

    def advance(at):
        s = cols[pl.ds(at, STEP)].astype(F32)
        tan = coef[live + 1 : live + 2]
        m = coef[0:1] * s
        for k in range(live):
            reach = 2**k
            if reach < 8:
                near[k, 8 : 8 + STEP] = s
                d = near[k, 8 - reach : 8 - reach + STEP]
                near[k, 0:8] = s[STEP - 8 :]
            elif reach < STEP:
                d = jnp.concatenate([hist[reach : 2 * reach], s[: STEP - reach]], 0)
                hist[reach : 2 * reach] = s[STEP - reach :]
            else:
                slot = pl.ds(pl.multiple_of(reach + lax.rem(at, reach), STEP), STEP)
                d = hist[slot]
                hist[slot] = s
            s = s + tan * d
            m = m + coef[k + 1 : k + 2] * s
        act[pl.ds(at, STEP)] = jax.nn.gelu(m).astype(BF16)

    left = z < 2

    @pl.loop(0, ways)
    def _(block):
        for a, b, steps in DURING:
            when = a if a == b else jnp.where(left, a, b)

            @pl.when(block == when)
            def _():
                relay(steps)

        @pl.when(block != me)
        def _():
            in_copy(block, block).wait_recv()

        @pl.when(block == me)
        def _():
            own_in.wait()

        @pl.loop(0, rows // STEP)
        def _(i):
            advance(pl.multiple_of(block * rows + i * STEP, STEP))

        @pl.when(block // (ways // 2) == side)
        def _():
            send_near(block, 0)

        @pl.when(block // (ways // 2) != side)
        def _():
            for c in range(EARLY):
                send_slice(block, c)

    for c in range(EARLY, DEEP):
        send_far(c)

    @pl.loop(0, ways // 2)
    def _(other):
        owner = side * (ways // 2) + lax.rem(me + other, ways // 2)
        for q in range(1, chunks):
            send_near(owner, q)

    relay(AFTER)

    def wait_bytes(ref, sem):
        pltpu.make_async_copy(ref, ref, sem).wait()

    def weights_here(i):
        own_w[i].wait()
        for p in range(i * PIECES, (i + 1) * PIECES):
            wait_bytes(wbuf.at[i, nx, pl.ds(0, 2 * quarter)], wc_recv.at[p])

    tiles = half // TILE

    def result_copy(q, tile):
        at = pl.ds(starts[q], sizes[q])
        lanes = pl.ds(pl.multiple_of(tile * TILE, TILE), TILE)
        return pltpu.make_async_remote_copy(
            src_ref=obuf.at[at, lanes],
            dst_ref=rbuf.at[at, lanes],
            send_sem=res_send,
            recv_sem=res_recv.at[q],
            device_id={"chan": nx},
            device_id_type=MESH,
        )

    def out_copy(q, owner):
        at = pl.ds(pl.multiple_of(owner * part + starts[q], 16), sizes[q])
        return pltpu.make_async_copy(done.at[at], out.at[at], out_sem)

    def sided(i, h, at, lanes, which):
        span = half // 2
        total_dot = None
        for source_x in range(2):
            deep = pl.ds(pl.multiple_of(source_x * half + which * span, span), span)
            dot = jnp.dot(piece[at, deep], wbuf[i, h, deep, lanes], preferred_element_type=F32)
            total_dot = dot if total_dot is None else total_dot + dot
        return total_dot

    def prepare():
        wait_bytes(piece.at[starts[WHOLE] :, 0:half], near_sem(WHOLE))
        at = pl.ds(starts[WHOLE], part - starts[WHOLE])
        for h in range(2):

            @pl.loop(0, tiles)
            def _(tile):
                lanes = pl.ds(pl.multiple_of(tile * TILE, TILE), TILE)
                for i in range(2):
                    sums[i, h * tiles + tile] = sided(i, h, at, lanes, side)

    def widen(q):
        at = pl.ds(starts[q], sizes[q])
        for c in range(SLICES):
            if starts[q] <= c * short < starts[q] + sizes[q]:
                wait_bytes(piece.at[0:short, 0:half], act_recv.at[c])
                if c + DEEP < SLICES:
                    send_far(c + DEEP)
        if q < WHOLE:
            wait_bytes(piece.at[at, 0:half], near_sem(q))
        if q == 0:
            weights_here(0)
            weights_here(1)

        for h in range(2):

            @pl.loop(0, tiles)
            def _(tile):
                lanes = pl.ds(pl.multiple_of(tile * TILE, TILE), TILE)
                if q < WHOLE:
                    value = jnp.dot(piece[at], wbuf[0, h, :, lanes], preferred_element_type=F32)
                    gate = jnp.dot(piece[at], wbuf[1, h, :, lanes], preferred_element_type=F32)
                else:
                    rest = pl.ds(starts[q] - starts[WHOLE], sizes[q])
                    value = sums[0, h * tiles + tile, rest] + sided(0, h, at, lanes, 1 - side)
                    gate = sums[1, h * tiles + tile, rest] + sided(1, h, at, lanes, 1 - side)
                to = pl.ds(pl.multiple_of(h * half + tile * TILE, TILE), TILE)
                hid[0 : sizes[q], to] = (value * jax.nn.sigmoid(gate)).astype(BF16)

    def project(q):
        @pl.loop(0, tiles)
        def _(tile):
            lanes = pl.ds(pl.multiple_of(tile * TILE, TILE), TILE)
            obuf[starts[q] : starts[q] + sizes[q], lanes] = jnp.dot(
                hid[0 : sizes[q]], wbuf[2, nx, :, lanes], preferred_element_type=F32
            ).astype(BF16)
            result_copy(q, tile).start()

        at = pl.ds(pl.multiple_of(x * part + starts[q], 16), sizes[q])

        @pl.loop(0, tiles)
        def _(tile):
            lanes = pl.ds(pl.multiple_of(tile * TILE, TILE), TILE)
            projected = jnp.dot(hid[0 : sizes[q]], wbuf[2, x, :, lanes], preferred_element_type=F32)
            done[at, lanes] = (projected + toks[at, lanes].astype(F32)).astype(BF16)

        out_copy(q, x).start()

    def finish(q):
        wait_bytes(rbuf.at[pl.ds(starts[q], sizes[q])], res_recv.at[q])
        base = nx * part + starts[q]

        @pl.loop(0, sizes[q] // 16)
        def _(i):
            at = pl.ds(pl.multiple_of(base + i * 16, 16), 16)
            got = rbuf[pl.ds(pl.multiple_of(starts[q] + i * 16, 16), 16)].astype(F32)
            done[at] = (got + toks[at].astype(F32)).astype(BF16)

        out_copy(q, nx).start()

    for q in range(chunks):
        widen(q)
        if q == 0:
            load.wait()
            weights_here(2)
        project(q)
        if q == WHOLE - 1:
            prepare()
    wait_bytes(cols.at[pl.ds(0, (ways - 1) * rows)], in_send)
    for p in range(count):
        x_copy(p).wait_send()
        if HOPS[p][0]:
            a_copy(p).wait_send()
        b_copy(p).wait_send()
        c_copy(p, False).wait_send()
        c_copy(p, True).wait_send()
    wait_bytes(act.at[pl.ds(0, (2 * ways - 1) * part)], act_send)
    for q in range(chunks):
        finish(q)
    wait_bytes(obuf, res_send)
    wait_bytes(done, out_sem)


def fused(tokens, low_angle, high_taps, level_mix, w_value, w_gate, out_weight):
    rows, half = tokens.shape
    depth = w_value.shape[0]
    ways = lax.axis_size(("seq", "sub"))
    total = rows * ways
    part = rows // 2
    chunk = part // 8 * max(EIGHTHS)
    chunks = len(EIGHTHS)
    vmem = pl.BlockSpec(memory_space=pltpu.VMEM)
    hbm = pl.BlockSpec(memory_space=pl.ANY)
    dma = pltpu.SemaphoreType.DMA
    return pl.pallas_call(
        functools.partial(kernel, ways),
        out_shape=jax.ShapeDtypeStruct((rows, half), BF16),
        in_specs=[hbm, vmem, vmem, vmem, hbm, hbm, hbm],
        out_specs=hbm,
        scratch_shapes=[
            pltpu.VMEM((rows, half), BF16),
            pltpu.VMEM((total, LANES), BF16),
            pltpu.VMEM((total, LANES), F32),
            pltpu.VMEM((3, STEP + 8, LANES), F32),
            pltpu.VMEM((level_mix.shape[0] + 7, LANES), F32),
            pltpu.VMEM((total, LANES), BF16),
            pltpu.VMEM((part, depth), BF16),
            pltpu.VMEM((chunk, depth), BF16),
            pltpu.VMEM((3, 2, depth, half), BF16),
            pltpu.VMEM((part, half), BF16),
            pltpu.VMEM((part, half), BF16),
            pltpu.VMEM((rows, half), BF16),
            pltpu.VMEM((2, 2 * half // TILE, part - part // 8 * sum(EIGHTHS[:WHOLE]), TILE), F32),
            dma((4,)),
            dma(()),
            dma((ways,)),
            dma((2,)),
            dma((3 * PIECES,)),
            dma((3 * PIECES,)),
            dma((3 * PIECES,)),
            dma((3 * PIECES,)),
            dma(()),
            dma((SLICES,)),
            dma((WHOLE + 1,)),
            dma(()),
            dma((chunks,)),
            dma(()),
        ],
        compiler_params=pltpu.CompilerParams(
            collective_id=0, has_side_effects=True, vmem_limit_bytes=50 * 1024 * 1024
        ),
        name="layer",
    )(tokens, low_angle[None], high_taps, level_mix, w_value, w_gate, out_weight)


def solution(mesh):
    shape = mesh.shape
    pair = shape["groups"] == 2 and shape["chan"] == 2 and shape["sub"] == 2 and shape["seq"] == 4
    ways = shape["seq"] * shape["sub"]

    def shards(tokens, *rest):
        rows, half = tokens.shape
        fits = half == ways * LANES and rows % STEP == 0 and rows % 256 == 0 and half % TILE == 0
        whole = rest[3].shape[0] == 2 * half and rows * ways * LANES <= 1 << 20
        body = fused if pair and fits and whole else plain
        return body(tokens, *rest)

    return jax.shard_map(
        shards,
        mesh=mesh,
        in_specs=(
            P(("groups", "seq", "sub"), "chan"),
            P("chan"),
            P(None, "chan"),
            P(None, "chan"),
            P(None, "chan"),
            P(None, "chan"),
            P(None, "chan"),
        ),
        out_specs=P(("groups", "seq", "sub"), "chan"),
        check_vma=False,
    )
```
